256 devices in a mesh: seq: 8 (over y, core), users: 32 (over x, z).
Axes of the slice: x: 4, y: 4, z: 8, core: 2. Of those that a mesh axis runs over, the one named last changes fastest.
Arguments:
- hidden: float32 [32, 8192, 512], P('users', 'seq'), may hold values from -256 to 256
- target: bfloat16 [32, 8192, 512], P('users', 'seq'), may hold values from -0.25 to 0.25
- pool_table: bfloat16 [8192, 512], P('users'), may hold values from -1 to 1
- pool_items: int32 [8192], P('users'), may hold values from 1 to 16383
- labels: int32 [32, 8192], P('users', 'seq'), may hold values from 1 to 16383
- chosen: int32 [32, 64, 8], P('users', 'seq'), may hold values from 0 to 31, all different within a row
- offsets: int32 [32, 5], P('users'), may hold values from 0 to 8192, as said below
Outputs:
- loss: float32 [], replicated
- grad_hidden: float32 [32, 8192, 512], P('users', 'seq')
- grad_table: float32 [8192, 512], P('users')
The draws below stay inside these ranges and needn't reach their ends.
Inputs may be any that keep to these rules, and one draw needn't show every extreme that they name: Each row offsets[u] starts at 0 and rises strictly; its last entry is the number of live positions of group u, and equals 8192 in some group; positions from it on are padding. `chosen`: each position block names 8 different negative blocks.
All inputs are finite; a program needn't handle non-finite values.
Results may differ from the reference program's by a relative error of at most 0.003.
Values may be sent and summed in bfloat16 or wider, within the bound.
A program may use at most 192 MiB of HBM per device.

```python
import math
import jax
import jax.numpy as jnp
from jax import lax

D = 512
NEG = 8192
NB = 256
KB = 8
PB = 128
HISTS = 4
ITEMS = 16384
USER_GROUPS = 32
GROUP_ROWS = 8192
GROUP_BLOCKS = 64
NEG_BLOCKS = 32


def common_direction(key):
    sub_key = jax.random.fold_in(key, 911)
    return jax.random.truncated_normal(sub_key, -3.0, 3.0, (D,), jnp.float32) / math.sqrt(D)


def draw_pool_table(key, part):
    direction = common_direction(key)
    key_base, key_hot = jax.random.split(jax.random.fold_in(key, 912), 2)
    base = jax.random.truncated_normal(key_base, -4.0, 4.0, (NEG, D), jnp.float32) / math.sqrt(D)
    hot_slot = jax.random.randint(key_hot, (NEG // NB,), 0, NB)
    is_hot = (jnp.arange(NB)[None, :] == hot_slot[:, None]).reshape(NEG, 1)
    rows = jnp.where(is_hot, direction[None, :] + 0.15 * base, base)
    return jnp.clip(rows, -1.0, 1.0).astype(jnp.bfloat16)


def draw_hidden(key, part):
    direction = common_direction(key)
    key_base, key_pick, key_power = jax.random.split(jax.random.fold_in(key, 913), 3)
    base = jax.random.truncated_normal(key_base, -6.0, 6.0, (USER_GROUPS, GROUP_ROWS, D), jnp.float32)
    planted = jax.random.randint(key_pick, (USER_GROUPS, GROUP_ROWS, 1), 0, 64) == 0
    power = jax.random.uniform(key_power, (USER_GROUPS, GROUP_ROWS, 1), jnp.float32, 120.0, 360.0)
    rows = jnp.where(planted, power * direction[None, None, :] + 0.05 * base, base)
    return jnp.clip(rows, -256.0, 256.0).astype(jnp.float32)


def draw_offsets(key, part):
    ceiling = GROUP_ROWS
    key_len, key_full, key_cut = jax.random.split(key, 3)
    totals = jax.random.randint(key_len, (USER_GROUPS,), ceiling // 8, ceiling + 1)
    fullest = jax.random.randint(key_full, (), 0, USER_GROUPS)
    totals = jnp.where(jnp.arange(USER_GROUPS) == fullest, ceiling, totals).astype(jnp.int32)
    draws_raw = jax.random.randint(key_cut, (USER_GROUPS, HISTS - 1), 0, 1 << 30)
    cut_points = draws_raw % (totals[:, None] - HISTS + 1)
    cut_points = jnp.sort(cut_points, axis=1) + jnp.arange(1, HISTS, dtype=jnp.int32)[None, :]
    leading = jnp.zeros((USER_GROUPS, 1), jnp.int32)
    return jnp.concatenate([leading, cut_points.astype(jnp.int32), totals[:, None]], axis=1).astype(jnp.int32)


def place_ends(array, own_key, smallest, largest):
    dims = array.shape
    place = [jax.random.randint(jax.random.fold_in(own_key, axis), (), 0, dims[axis]) for axis in range(len(dims))]
    array = array.at[tuple(place)].set(smallest)
    longest = dims.index(max(dims))
    place[longest] = (place[longest] + 1) % dims[longest]
    return array.at[tuple(place)].set(largest)


def levels(own_key, shape, cuts, low, top_value):
    def one(dim, parts):
        draws = jax.random.uniform(jax.random.fold_in(jax.random.fold_in(own_key, 6), dim), (parts,), jnp.float32, low / len(cuts), top_value / len(cuts))
        return jnp.repeat(jnp.exp(draws), shape[dim] // parts).reshape((-1,) + (1,) * (len(shape) - dim - 1))

    loudness = one(*cuts[0])
    for cut in cuts[1:]:
        loudness = loudness * one(*cut)
    return loudness


def choose_distinct(key, rows, count, top, lift):
    sequence = jax.random.permutation(jax.random.fold_in(key, 1), count)
    boost = sequence
    for power in range(3):
        boost = boost * boost // count
    boost = boost * lift // count
    lots = jax.random.randint(jax.random.fold_in(key, 2), (rows, count), 0, 4096) + boost
    sure = jax.random.permutation(jax.random.fold_in(key, 3), rows)[jnp.arange(count) % rows]
    lots = jnp.where(jnp.arange(rows)[:, None] == sure[None, :], 1 << 14, lots)
    score = lots * count + jnp.arange(count)
    return lax.top_k(score.astype(jnp.int32), top)[1].astype(jnp.int32)


def gaussian(rng, extent, scale, bound, cuts=(), kind=jnp.bfloat16):
    result = scale * jax.random.normal(rng, extent, jnp.float32)
    if cuts:
        result = result * levels(rng, extent, cuts, -0.22, 0.18)
    return jnp.clip(result, -bound, bound).astype(kind)


def setup_inputs(seed: int = 0) -> dict:
    splits = jax.random.split(jax.random.key(seed), 8)
    hidden = draw_hidden(jax.random.fold_in(splits[7], 71), 0)
    target = gaussian(splits[1], (USER_GROUPS, GROUP_ROWS, D), D ** -0.5, 0.25, ((0, 32), (1, 8)))
    pool_table = draw_pool_table(jax.random.fold_in(splits[7], 71), 0)
    pool_items = place_ends(jax.random.randint(splits[3], (NEG,), 1, ITEMS), jax.random.fold_in(splits[3], 1), 1, ITEMS - 1).astype(jnp.int32)
    labels = place_ends(jax.random.randint(splits[4], (USER_GROUPS, GROUP_ROWS), 1, ITEMS), jax.random.fold_in(splits[4], 1), 1, ITEMS - 1).astype(jnp.int32)
    chosen = choose_distinct(splits[5], USER_GROUPS * GROUP_BLOCKS, NEG_BLOCKS, KB, 2048).reshape((USER_GROUPS, GROUP_BLOCKS, KB))
    offsets = draw_offsets(jax.random.fold_in(splits[7], 71), 0)
    return dict(hidden=hidden, target=target, pool_table=pool_table, pool_items=pool_items, labels=labels, chosen=chosen, offsets=offsets)


def history_weights(bounds, positions):
    starts = bounds[:-1]
    finish = bounds[1:]
    lengths = (finish - starts).astype(jnp.float32)
    inside = (positions[..., None] >= starts) & (positions[..., None] < finish)
    return jnp.sum(jnp.where(inside, 1.0 / lengths, 0.0), axis=-1).astype(jnp.float32)


def block_terms(states, target, labels, weights, chosen, pool_rows, pool_ids, factor):
    narrow = states.astype(jnp.bfloat16)
    negatives = jnp.take(pool_rows, chosen, axis=0).reshape(-1, pool_rows.shape[2])
    neg_items = jnp.take(pool_ids, chosen, axis=0).reshape(-1)
    scores = jnp.dot(narrow, negatives.T, preferred_element_type=jnp.float32)
    target_wide = target.astype(jnp.float32)
    positive = jnp.sum(narrow.astype(jnp.float32) * target_wide, axis=1)
    masked = jnp.where(neg_items[None, :] == labels[:, None], -1e30, scores)
    peak = jnp.maximum(positive, jnp.max(masked, axis=1))
    neg_exp = jnp.exp(masked - peak[:, None])
    pos_exp = jnp.exp(positive - peak)
    totals = pos_exp + jnp.sum(neg_exp, axis=1)
    cross = peak + jnp.log(totals) - positive
    coeff = weights * factor
    neg_grad = (coeff[:, None] * neg_exp / totals[:, None]).astype(jnp.bfloat16)
    pos_grad = coeff * (pos_exp / totals - 1.0)
    state_grad = jnp.dot(neg_grad, negatives, preferred_element_type=jnp.float32) + pos_grad[:, None] * target_wide
    pool_grad = jnp.dot(neg_grad.T, narrow, preferred_element_type=jnp.float32)
    pool_grad = pool_grad.reshape(chosen.shape[0], pool_rows.shape[1], pool_rows.shape[2])
    return jnp.sum(weights * cross), state_grad, pool_grad


def reference(hidden, target, pool_table, pool_items, labels, chosen, offsets):
    groups = hidden.shape[0]
    length = hidden.shape[1]
    positions = jnp.arange(length, dtype=jnp.int32)
    weights = jax.vmap(history_weights, in_axes=(0, None))(offsets, positions)
    factor = 1.0 / (groups * (offsets.shape[1] - 1))
    pool_rows = pool_table.reshape(NEG // NB, NB, D)
    pool_ids = pool_items.reshape(NEG // NB, NB)
    sliced = (hidden.reshape(-1, PB, D), target.reshape(-1, PB, D), labels.reshape(-1, PB),
              weights.reshape(-1, PB), chosen.reshape(-1, KB))

    def advance(carried, slices):
        loss_acc, grad_acc = carried
        part_loss, state_grad, pool_grad = block_terms(slices[0], slices[1], slices[2], slices[3], slices[4], pool_rows, pool_ids, factor)
        return (loss_acc + part_loss, grad_acc.at[slices[4]].add(pool_grad)), state_grad

    initial = (jnp.zeros((), jnp.float32), jnp.zeros((NEG // NB, NB, D), jnp.float32))
    (loss_acc, grad_acc), state_grads = lax.scan(advance, initial, sliced)
    return loss_acc * factor, state_grads.reshape(hidden.shape), grad_acc.reshape(NEG, D)
```

```python
import functools
import jax
import jax.numpy as jnp
from jax import lax
from jax.experimental import pallas as pl
from jax.experimental.pallas import tpu as pltpu
from jax.sharding import PartitionSpec as P

MESH = pl.DeviceIdType.MESH
NX, NY, NZ = 4, 4, 8


def where_am_i():
    seq, users = lax.axis_index("seq"), lax.axis_index("users")
    return users // NZ, seq // 2, users % NZ, seq % 2


def device(x, y, z, c):
    return {"seq": y * 2 + c, "users": x * NZ + z}


def greet(peers):
    barrier = pltpu.get_barrier_semaphore()
    for peer in peers:
        pl.semaphore_signal(barrier, inc=1, device_id=peer, device_id_type=MESH)
    pl.semaphore_wait(barrier, len(peers))


def push(src, dst, send_sem, recv_sem, to):
    copy = pltpu.make_async_remote_copy(src_ref=src, dst_ref=dst, send_sem=send_sem, recv_sem=recv_sem,
                                        device_id=to, device_id_type=MESH)
    copy.start()
    return copy


def gather_kernel(shard, items, table, all_items, local_sem, partner_send, partner_recv, item_send, item_recv,
                  send1, recv1, send2, recv2):
    x, y, z, c = where_am_i()
    users = x * NZ + z
    total = NX * NZ
    quarter = shard.shape[1] // 2
    others = [lax.rem(users + d, total) for d in range(1, total)]
    partner = device(x, y, z, 1 - c)
    greet([{"seq": y * 2 + c, "users": u} for u in others] + [partner])

    mine = pltpu.make_async_copy(shard, table.at[users], local_sem.at[0])
    mine.start()
    mine_items = pltpu.make_async_copy(items, all_items.at[users], local_sem.at[1])
    mine_items.start()

    def run(n1, n2, me1, me2, region, dev):
        copies, pending = [], {}

        def part(ref, s, n, d):
            return ref if s < n // 2 else ref.at[pl.ds(0 if d > 0 else quarter, quarter)]

        def size(ring):
            return n1 if ring == 1 else n2

        def place(ring, sub, back):
            if ring == 1:
                return lax.rem(me1 - back + n1, n1), me2
            return lax.rem(me1 + sub + n1, n1), lax.rem(me2 - back + n2, n2)

        def send(ring, sub, s, d):
            n = size(ring)
            dst = region(*place(ring, sub, d * (s - 1)))
            src = shard.at[c] if s == 1 and sub == 0 else dst
            if ring == 1:
                k = (s - 1) * 2 + (d < 0)
                sems, to = (send1.at[k], recv1.at[k]), dev(lax.rem(me1 + d + n, n), me2)
            else:
                k = ((sub % n1) * (n2 // 2) + s - 1) * 2 + (d < 0)
                sems, to = (send2.at[k], recv2.at[k]), dev(me1, lax.rem(me2 + d + n, n))
            copy = push(part(src, s, n, d), part(dst, s, n, d), *sems, to)
            copies.append(copy)
            pending[ring, sub, s, d] = copy

        passed = []

        def arrive(ring, sub, s, d):
            pending.pop((ring, sub, s, d)).wait_recv()
            ref = part(region(*place(ring, sub, d * s)), s, size(ring), d)
            passed.append(push(ref, ref, partner_send.at[len(passed)], partner_recv, partner))

        ready = {0: 0}
        for s in range(1, n1 // 2):
            ready[-s], ready[s] = s, s
        ready[n1 // 2] = n1 // 2
        for time in range(1, n1 // 2 + n2 // 2 + 2):
            if time <= n1 // 2 + 1:
                for d in (1, -1):
                    if time > 1:
                        arrive(1, 0, time - 1, d)
                    if time <= n1 // 2:
                        send(1, 0, time, d)
            for sub, at in ready.items():
                s = time - at
                if 1 <= s <= n2 // 2 + 1:
                    for d in (1, -1):
                        if s > 1:
                            arrive(2, sub, s - 1, d)
                        if s <= n2 // 2:
                            send(2, sub, s, d)
        assert not pending
        for copy in copies + passed:
            copy.wait_send()

    shared = [push(items, all_items.at[users], item_send.at[d], item_recv, {"seq": y * 2 + c, "users": u})
              for d, u in enumerate(others)]

    @pl.when(c == 0)
    def _():
        run(NX, NZ, x, z, lambda i1, i2: table.at[i1 * NZ + i2, 0], lambda i1, i2: device(i1, y, i2, 0))

    @pl.when(c == 1)
    def _():
        run(NZ, NX, z, x, lambda i1, i2: table.at[i2 * NZ + i1, 1], lambda i1, i2: device(i2, y, i1, 1))

    for copy in shared:
        copy.wait_send()
    rest = all_items.at[pl.ds(0, total - 1)]
    pltpu.make_async_copy(rest, rest, item_recv).wait()
    rest = table.at[pl.ds(0, total - 1), 0]
    pltpu.make_async_copy(rest, rest, partner_recv).wait()
    mine.wait()
    mine_items.wait()


def gather(pool_table, pool_items):
    rows, features = pool_table.shape
    total = NX * NZ
    dma = pltpu.SemaphoreType.DMA
    anywhere = pl.BlockSpec(memory_space=pl.ANY)
    table, items = pl.pallas_call(
        gather_kernel,
        in_specs=[pl.BlockSpec(memory_space=pltpu.VMEM)] * 2,
        out_specs=[anywhere, anywhere],
        out_shape=(
            jax.ShapeDtypeStruct((total, 2, rows // 2, features), pool_table.dtype),
            jax.ShapeDtypeStruct((total, 1, rows), pool_items.dtype),
        ),
        scratch_shapes=[dma((2,)), dma((40,)), dma, dma((total - 1,)), dma, dma((8,)), dma((8,)), dma((32,)),
                        dma((32,))],
        compiler_params=pltpu.CompilerParams(collective_id=0, has_side_effects=True),
        name="gather",
    )(pool_table.reshape(2, rows // 2, features), pool_items.reshape(1, rows))
    return table.reshape(total, rows, features), items


NB = 256
PB = 128


def score_kernel(chosen_s, offsets_s, place_s, hidden_ref, target_ref, labels_ref, table_ref, items_ref,
                 gh_ref, loss_ref, gt_hbm, acc, scores, grads, loss_acc, sem, *, factor):
    b = pl.program_id(0)
    blocks = pl.num_programs(0)
    features = hidden_ref.shape[1]
    kb = chosen_s.shape[1]
    hists = offsets_s.shape[0] - 1
    base = place_s[0] + b * PB

    @pl.when(b == 0)
    def _():
        loss_acc[...] = jnp.zeros_like(loss_acc)

        @pl.loop(0, acc.shape[0])
        def _(k):
            acc[k] = jnp.zeros(acc.shape[1:], acc.dtype)

    live = base < offsets_s[hists]

    @pl.when(jnp.logical_not(live))
    def _():
        gh_ref[...] = jnp.zeros_like(gh_ref)

    @pl.when(live)
    def _():
        narrow = hidden_ref[...].astype(jnp.bfloat16)
        target_wide = target_ref[...].astype(jnp.float32)
        positive = jnp.sum(narrow.astype(jnp.float32) * target_wide, axis=1, keepdims=True)
        labels = jnp.broadcast_to(labels_ref[0], (PB, PB)).T[:, :1]
        positions = base + lax.broadcasted_iota(jnp.int32, (PB, 1), 0)
        weights = jnp.zeros((PB, 1), jnp.float32)
        for h in range(hists):
            start, finish = offsets_s[h], offsets_s[h + 1]
            length = jnp.broadcast_to(finish - start, (PB, 1)).astype(jnp.float32)
            inside = (positions >= start) & (positions < finish)
            weights = weights + jnp.where(inside, 1.0 / length, 0.0)

        top = jnp.full((PB, 128), -1e30, jnp.float32)
        for j in range(kb):
            k = chosen_s[b, j]
            raw = lax.dot_general(narrow, table_ref[k], (((1,), (1,)), ((), ())),
                                  preferred_element_type=jnp.float32)
            masked = jnp.where(items_ref[k] == labels, -1e30, raw)
            scores[:, j * NB:(j + 1) * NB] = masked
            for i in range(NB // 128):
                top = jnp.maximum(top, masked[:, i * 128:(i + 1) * 128])
        peak = jnp.maximum(positive, jnp.max(top, axis=1, keepdims=True))
        added = jnp.zeros((PB, 128), jnp.float32)
        for j in range(kb):
            each = jnp.exp(scores[:, j * NB:(j + 1) * NB] - peak)
            scores[:, j * NB:(j + 1) * NB] = each
            for i in range(NB // 128):
                added = added + each[:, i * 128:(i + 1) * 128]
        pos_exp = jnp.exp(positive - peak)
        totals = pos_exp + jnp.sum(added, axis=1, keepdims=True)
        cross = peak + jnp.log(totals) - positive
        loss_acc[...] += jnp.broadcast_to(jnp.sum(weights * cross, axis=0, keepdims=True), loss_acc.shape)
        coeff = weights * factor
        scale = coeff / totals
        pos_grad = coeff * (pos_exp / totals - 1.0)
        for j in range(kb):
            grads[:, j * NB:(j + 1) * NB] = (scores[:, j * NB:(j + 1) * NB] * scale).astype(jnp.bfloat16)
        out = pos_grad * target_wide
        for j in range(kb):
            k = chosen_s[b, j]
            g = grads[:, j * NB:(j + 1) * NB]
            out = out + jnp.dot(g, table_ref[k], preferred_element_type=jnp.float32)
            acc[k] += lax.dot_general(g, narrow, (((0,), (0,)), ((), ())), preferred_element_type=jnp.float32)
        gh_ref[...] = out

    @pl.when(b == blocks - 1)
    def _():
        loss_ref[...] = loss_acc[...]
        copy = pltpu.make_async_copy(acc, gt_hbm, sem)
        copy.start()
        copy.wait()


def score(hidden, target, labels, chosen, offsets, place, table, items, factor):
    rows, features = hidden.shape
    blocks = rows // PB
    count = table.shape[0]
    kb = chosen.shape[1]
    one = pl.Buffered(1)
    grid_spec = pltpu.PrefetchScalarGridSpec(
        num_scalar_prefetch=3,
        grid=(blocks,),
        in_specs=[
            pl.BlockSpec((PB, features), lambda b, *_: (b, 0)),
            pl.BlockSpec((PB, features), lambda b, *_: (b, 0)),
            pl.BlockSpec((1, 1, PB), lambda b, *_: (b, 0, 0)),
            pl.BlockSpec((count, NB, features), lambda b, *_: (0, 0, 0), pipeline_mode=one),
            pl.BlockSpec((count, 1, NB), lambda b, *_: (0, 0, 0), pipeline_mode=one),
        ],
        out_specs=[
            pl.BlockSpec((PB, features), lambda b, *_: (b, 0)),
            pl.BlockSpec((8, 128), lambda b, *_: (0, 0)),
            pl.BlockSpec(memory_space=pl.ANY),
        ],
        scratch_shapes=[
            pltpu.VMEM((count, NB, features), jnp.float32),
            pltpu.VMEM((PB, kb * NB), jnp.float32),
            pltpu.VMEM((PB, kb * NB), jnp.bfloat16),
            pltpu.VMEM((8, 128), jnp.float32),
            pltpu.SemaphoreType.DMA,
        ],
    )
    return pl.pallas_call(
        functools.partial(score_kernel, factor=factor),
        grid_spec=grid_spec,
        out_shape=(
            jax.ShapeDtypeStruct((rows, features), jnp.float32),
            jax.ShapeDtypeStruct((8, 128), jnp.float32),
            jax.ShapeDtypeStruct((count, NB, features), jnp.float32),
        ),
        compiler_params=pltpu.CompilerParams(vmem_limit_bytes=48 << 20),
        name="score",
    )(chosen, offsets, place, hidden, target, labels.reshape(blocks, 1, PB), table, items)


def reduce_kernel(grads, loss_in, out, loss_out, own, first, half_up, half_down, full_up, full_down,
                  chunk_half_up, chunk_half_down, chunk_up, chunk_down, tail_up, tail_down, parts, sums,
                  load_sem, pair_send, pair_recv, s1, r1, s2, r2, s3, r3, s4, r4, s5, r5, loss_send, loss_recv):
    x, y, z, c = where_am_i()
    me1 = y * (1 - c) + x * c
    me2 = x * (1 - c) + y * c
    partner = device(x, y, z, 1 - c)

    def dev(i1, i2, iz):
        return device(i2 * (1 - c) + i1 * c, i1 * (1 - c) + i2 * c, iz, c)

    xs = [device(lax.rem(x + d, NX), y, z, c) for d in range(1, NX)]
    ys = [device(x, lax.rem(y + d, NY), z, c) for d in range(1, NY)]
    zs = [device(x, y, lax.rem(z + d, NZ), c) for d in range(1, NZ)]
    greet([partner] + xs + ys + zs)
    sent = []

    def unit(core, i1, i2):
        return grads.at[i2 * (1 - core) + i1 * core, :, core, i1 * (1 - core) + i2 * core]

    order = [(2, 0), (2, 1), (1, 1), (3, 0), (1, 0), (3, 1), (0, 0), (0, 1)]
    other1 = x * (1 - c) + y * c
    pair, load = {}, {}
    slot = 0
    for d, h in order:
        for q in (2 * h, 2 * h + 1):
            p = lax.rem(other1 + d, 4)
            copy = push(unit(1 - c, p, q), first.at[p, q], pair_send.at[slot], pair_recv.at[slot], partner)
            sent.append(copy)
            p = lax.rem(me1 + d, 4)
            here = pltpu.make_async_copy(unit(c, p, q), own.at[p, q], load_sem.at[slot])
            here.start()
            pair[d, q], load[d, q] = copy, here
            slot += 1

    def loss_round(k, base, count, me, peers):
        parts[base + me] = sums[...]
        copies = []
        for d, peer in enumerate(peers):
            copies.append(push(sums, parts.at[base + me], loss_send.at[k + d], loss_recv.at[k + d], peer))
        return copies

    def loss_sum(copies, base, count):
        for copy in copies:
            copy.wait()
        total = parts[base]
        for i in range(1, count):
            total = total + parts[base + i]
        sums[...] = total

    sums[...] = loss_in[...]
    rounds = loss_round(0, 0, 2, c, [partner])

    def together(d, h):
        p = lax.rem(me1 + d, 4)
        for q in (2 * h, 2 * h + 1):
            pair[d, q].wait_recv()
            load[d, q].wait()

            @pl.loop(0, NZ)
            def _(i):
                own[p, q, i] += first[p, q, i]

    def add(dst, src, count):
        @pl.loop(0, count)
        def _(i):
            dst[i] += src[i]

    up1, down1 = dev(lax.rem(me1 + 1, 4), me2, z), dev(lax.rem(me1 + 3, 4), me2, z)
    opposite, above, below = lax.rem(me1 + 2, 4), lax.rem(me1 + 1, 4), lax.rem(me1 + 3, 4)

    def half(ref, h, size):
        return ref.at[pl.ds(h * size, size)]

    together(2, 0)
    a_up = push(half(own.at[opposite], 0, 2), half_up, s1.at[0], r1.at[0], up1)
    together(2, 1)
    a_down = push(half(own.at[opposite], 1, 2), half_down, s1.at[1], r1.at[1], down1)
    together(1, 1)
    b_up = push(half(own.at[above], 1, 2), half(full_up, 1, 2), s1.at[2], r1.at[2], up1)
    together(3, 0)
    b_down = push(half(own.at[below], 0, 2), half(full_down, 0, 2), s1.at[3], r1.at[3], down1)
    together(1, 0)
    together(3, 1)

    def add_units(p, h, ref, base):
        for q in range(2):
            @pl.loop(0, NZ)
            def _(i):
                own[p, 2 * h + q, i] += ref[base + q, i]

    a_up.wait_recv()
    add_units(above, 0, half_up, 0)
    c_up = push(half(own.at[above], 0, 2), half(full_up, 0, 2), s1.at[4], r1.at[4], up1)
    a_down.wait_recv()
    add_units(below, 1, half_down, 0)
    c_down = push(half(own.at[below], 1, 2), half(full_down, 1, 2), s1.at[5], r1.at[5], down1)
    sent += [a_up, a_down, b_up, b_down, c_up, c_down]
    together(0, 0)
    together(0, 1)
    loss_sum(rounds, 0, 2)
    rounds = loss_round(1, 2, NY, y, ys)
    b_up.wait_recv()
    add_units(me1, 1, full_up, 2)
    b_down.wait_recv()
    add_units(me1, 0, full_down, 0)
    c_up.wait_recv()
    add_units(me1, 0, full_up, 0)
    c_down.wait_recv()
    add_units(me1, 1, full_down, 2)

    mine = own.at[me1]
    up2, down2 = dev(me1, lax.rem(me2 + 1, 4), z), dev(me1, lax.rem(me2 + 3, 4), z)
    opposite, above, below = lax.rem(me2 + 2, 4), lax.rem(me2 + 1, 4), lax.rem(me2 + 3, 4)
    a_up = push(half(mine.at[opposite], 0, 4), chunk_half_up, s2.at[0], r2.at[0], up2)
    a_down = push(half(mine.at[opposite], 1, 4), chunk_half_down, s2.at[1], r2.at[1], down2)
    b_up = push(half(mine.at[above], 1, 4), half(chunk_up, 1, 4), s2.at[2], r2.at[2], up2)
    b_down = push(half(mine.at[below], 0, 4), half(chunk_down, 0, 4), s2.at[3], r2.at[3], down2)
    loss_sum(rounds, 2, NY)
    rounds = loss_round(4, 6, NX, x, xs)
    a_up.wait_recv()
    add(half(mine.at[above], 0, 4), chunk_half_up, 4)
    c_up = push(half(mine.at[above], 0, 4), half(chunk_up, 0, 4), s2.at[4], r2.at[4], up2)
    a_down.wait_recv()
    add(half(mine.at[below], 1, 4), chunk_half_down, 4)
    c_down = push(half(mine.at[below], 1, 4), half(chunk_down, 1, 4), s2.at[5], r2.at[5], down2)
    sent += [a_up, a_down, b_up, b_down, c_up, c_down]
    here = mine.at[me2]
    b_up.wait_recv()
    add(half(here, 1, 4), half(chunk_up, 1, 4), 4)
    b_down.wait_recv()
    add(half(here, 0, 4), half(chunk_down, 0, 4), 4)
    c_up.wait_recv()
    add(half(here, 0, 4), half(chunk_up, 0, 4), 4)
    c_down.wait_recv()
    add(half(here, 1, 4), half(chunk_down, 1, 4), 4)
    loss_sum(rounds, 6, NX)
    rounds = loss_round(7, 10, NZ, z, zs)

    up3, down3 = dev(me1, me2, lax.rem(z + 1, NZ)), dev(me1, me2, lax.rem(z + NZ - 1, NZ))
    rows = own.shape[3]
    for s in range(1, NZ // 2 + 1):
        ahead = NZ // 2 + 1 - s
        goes_up, goes_down = lax.rem(z + ahead, NZ), lax.rem(z + NZ - ahead, NZ)
        if s == 1:
            u_src, u_dst = half(here.at[goes_up], 0, rows // 2), half(tail_up.at[0], 0, rows // 2)
            d_src, d_dst = half(here.at[goes_down], 1, rows // 2), half(tail_down.at[0], 1, rows // 2)
        else:
            u_src, u_dst, d_src, d_dst = here.at[goes_up], tail_up.at[s - 1], here.at[goes_down], tail_down.at[s - 1]
        u = push(u_src, u_dst, s3.at[2 * s - 2], r3.at[2 * s - 2], up3)
        d = push(d_src, d_dst, s3.at[2 * s - 1], r3.at[2 * s - 1], down3)
        sent += [u, d]
        into_up, into_down = lax.rem(z + ahead - 1, NZ), lax.rem(z + NZ - ahead + 1, NZ)
        u.wait_recv()
        if s == 1:
            here[into_up, : rows // 2] += tail_up[0, : rows // 2]
        else:
            here[into_up] += tail_up[s - 1]
        d.wait_recv()
        if s == 1:
            here[into_down, rows // 2 :] += tail_down[0, rows // 2 :]
        else:
            here[into_down] += tail_down[s - 1]

    out[c, y] = here[z]
    done = out.at[c, y]
    copies = [push(here.at[z], done, s4.at[0], r4.at[0], partner)]
    spread = [push(here.at[z], done, s4.at[d], r4.at[d], peer) for d, peer in enumerate(ys, 1)]
    sent += copies + spread
    loss_sum(rounds, 10, NZ)
    loss_out[...] = sums[...]
    for d, copy in enumerate(spread, 1):
        copy.wait_recv()
        ref = out.at[c, lax.rem(y + NY - d, NY)]
        copies.append(push(ref, ref, s5.at[d - 1], r5.at[d - 1], partner))
        sent.append(copies[-1])
    for copy in copies:
        copy.wait_recv()
    for copy in sent:
        copy.wait_send()


def reduce_rows(grads, loss):
    total, rows, features = grads.shape
    sub = rows // (2 * NY)
    dma = pltpu.SemaphoreType.DMA
    f32 = jnp.float32
    out, loss = pl.pallas_call(
        reduce_kernel,
        in_specs=[pl.BlockSpec(memory_space=pl.ANY), pl.BlockSpec(memory_space=pltpu.VMEM)],
        out_specs=[pl.BlockSpec(memory_space=pltpu.VMEM)] * 2,
        out_shape=(jax.ShapeDtypeStruct((2, NY, sub, features), f32), jax.ShapeDtypeStruct(loss.shape, f32)),
        scratch_shapes=[
            pltpu.VMEM((4, 4, NZ, sub, features), f32),
            pltpu.VMEM((4, 4, NZ, sub, features), f32),
            pltpu.VMEM((2, NZ, sub, features), f32),
            pltpu.VMEM((2, NZ, sub, features), f32),
            pltpu.VMEM((4, NZ, sub, features), f32),
            pltpu.VMEM((4, NZ, sub, features), f32),
            pltpu.VMEM((NZ // 2, sub, features), f32),
            pltpu.VMEM((NZ // 2, sub, features), f32),
            pltpu.VMEM((NZ, sub, features), f32),
            pltpu.VMEM((NZ, sub, features), f32),
            pltpu.VMEM((NZ // 2, sub, features), f32),
            pltpu.VMEM((NZ // 2, sub, features), f32),
            pltpu.VMEM((2 + NY + NX + NZ,) + loss.shape, f32),
            pltpu.VMEM(loss.shape, f32),
            dma((16,)), dma((16,)), dma((16,)),
            dma((6,)), dma((6,)), dma((6,)), dma((6,)), dma((8,)), dma((8,)),
            dma((4,)), dma((4,)), dma((3,)), dma((3,)), dma((14,)), dma((14,)),
        ],
        compiler_params=pltpu.CompilerParams(collective_id=1, has_side_effects=True, vmem_limit_bytes=48 << 20),
        name="reduce",
    )(grads.reshape(NX, NZ, 2, NY, sub, features), loss)
    return out.reshape(rows, features), loss[0, 0]


def per_device(hidden, target, pool_table, pool_items, labels, chosen, offsets):
    user_count = lax.axis_size("users")
    length, features = hidden.shape[1:]
    factor = 1.0 / (user_count * (offsets.shape[1] - 1))
    table, items = gather(pool_table, pool_items)
    place = (lax.axis_index("seq") * length).reshape(1)
    grad_hidden, loss, grads = score(
        hidden[0], target[0], labels[0], chosen[0], offsets[0], place, table, items, factor
    )
    grad_table, loss_total = reduce_rows(grads, loss)
    return (loss_total * factor, grad_hidden[None], grad_table)


def solution(mesh):
    return jax.shard_map(
        per_device,
        mesh=mesh,
        in_specs=(
            P("users", "seq", None),
            P("users", "seq", None),
            P("users", None),
            P("users"),
            P("users", "seq"),
            P("users", "seq", None),
            P("users", None),
        ),
        out_specs=(P(), P("users", "seq", None), P("users", None)),
        check_vma=False,
    )
```

```python
import functools
import jax
import jax.numpy as jnp
from jax import lax
from jax.experimental import pallas as pl
from jax.experimental.pallas import tpu as pltpu
from jax.sharding import PartitionSpec as P

MESH = pl.DeviceIdType.MESH
NX, NY, NZ = 4, 4, 8


def where_am_i():
    seq, users = lax.axis_index("seq"), lax.axis_index("users")
    return users // NZ, seq // 2, users % NZ, seq % 2


def device(x, y, z, c):
    return {"seq": y * 2 + c, "users": x * NZ + z}


def greet(peers):
    barrier = pltpu.get_barrier_semaphore()
    for peer in peers:
        pl.semaphore_signal(barrier, inc=1, device_id=peer, device_id_type=MESH)
    pl.semaphore_wait(barrier, len(peers))


def push(src, dst, send_sem, recv_sem, to):
    copy = pltpu.make_async_remote_copy(src_ref=src, dst_ref=dst, send_sem=send_sem, recv_sem=recv_sem,
                                        device_id=to, device_id_type=MESH)
    copy.start()
    return copy


def gather_kernel(shard, items, chosen, table, all_items, both, local_sem, pair_sem, partner_send, partner_recv,
                  item_send, item_recv, send1, recv1, send2, recv2):
    x, y, z, c = where_am_i()
    users = x * NZ + z
    total = NX * NZ
    quarter = shard.shape[1] // 2
    others = [lax.rem(users + d, total) for d in range(1, total)]
    partner = device(x, y, z, 1 - c)
    greet([{"seq": y * 2 + c, "users": u} for u in others] + [partner])

    mine = pltpu.make_async_copy(shard, table.at[users], local_sem.at[0])
    mine.start()
    mine_items = pltpu.make_async_copy(items, all_items.at[users], local_sem.at[1])
    mine_items.start()
    mine_chosen = pltpu.make_async_copy(chosen, both.at[c], local_sem.at[2])
    mine_chosen.start()
    theirs = push(chosen, both.at[c], pair_sem.at[0], pair_sem.at[1], partner)

    def run(n1, n2, me1, me2, region, dev):
        copies, pending = [], {}

        def part(ref, s, n, d):
            return ref if s < n // 2 else ref.at[pl.ds(0 if d > 0 else quarter, quarter)]

        def size(ring):
            return n1 if ring == 1 else n2

        def place(ring, sub, back):
            if ring == 1:
                return lax.rem(me1 - back + n1, n1), me2
            return lax.rem(me1 + sub + n1, n1), lax.rem(me2 - back + n2, n2)

        def send(ring, sub, s, d):
            n = size(ring)
            dst = region(*place(ring, sub, d * (s - 1)))
            src = shard.at[c] if s == 1 and sub == 0 else dst
            if ring == 1:
                k = (s - 1) * 2 + (d < 0)
                sems, to = (send1.at[k], recv1.at[k]), dev(lax.rem(me1 + d + n, n), me2)
            else:
                k = ((sub % n1) * (n2 // 2) + s - 1) * 2 + (d < 0)
                sems, to = (send2.at[k], recv2.at[k]), dev(me1, lax.rem(me2 + d + n, n))
            copy = push(part(src, s, n, d), part(dst, s, n, d), *sems, to)
            copies.append(copy)
            pending[ring, sub, s, d] = copy

        passed = []

        def arrive(ring, sub, s, d):
            pending.pop((ring, sub, s, d)).wait_recv()
            ref = part(region(*place(ring, sub, d * s)), s, size(ring), d)
            passed.append(push(ref, ref, partner_send.at[len(passed)], partner_recv, partner))

        ready = {0: 0}
        for s in range(1, n1 // 2):
            ready[-s], ready[s] = s, s
        ready[n1 // 2] = n1 // 2
        for time in range(1, n1 // 2 + n2 // 2 + 2):
            if time <= n1 // 2 + 1:
                for d in (1, -1):
                    if time > 1:
                        arrive(1, 0, time - 1, d)
                    if time <= n1 // 2:
                        send(1, 0, time, d)
            for sub, at in ready.items():
                s = time - at
                if 1 <= s <= n2 // 2 + 1:
                    for d in (1, -1):
                        if s > 1:
                            arrive(2, sub, s - 1, d)
                        if s <= n2 // 2:
                            send(2, sub, s, d)
        assert not pending
        for copy in copies + passed:
            copy.wait_send()

    shared = [push(items, all_items.at[users], item_send.at[d], item_recv, {"seq": y * 2 + c, "users": u})
              for d, u in enumerate(others)]

    @pl.when(c == 0)
    def _():
        run(NX, NZ, x, z, lambda i1, i2: table.at[i1 * NZ + i2, 0], lambda i1, i2: device(i1, y, i2, 0))

    @pl.when(c == 1)
    def _():
        run(NZ, NX, z, x, lambda i1, i2: table.at[i2 * NZ + i1, 1], lambda i1, i2: device(i2, y, i1, 1))

    for copy in shared:
        copy.wait_send()
    rest = all_items.at[pl.ds(0, total - 1)]
    pltpu.make_async_copy(rest, rest, item_recv).wait()
    rest = table.at[pl.ds(0, total - 1), 0]
    pltpu.make_async_copy(rest, rest, partner_recv).wait()
    mine.wait()
    mine_items.wait()
    mine_chosen.wait()
    theirs.wait()


def gather(pool_table, pool_items, chosen):
    rows, features = pool_table.shape
    total = NX * NZ
    dma = pltpu.SemaphoreType.DMA
    anywhere = pl.BlockSpec(memory_space=pl.ANY)
    table, items, both = pl.pallas_call(
        gather_kernel,
        in_specs=[pl.BlockSpec(memory_space=pltpu.VMEM)] * 3,
        out_specs=[anywhere] * 3,
        out_shape=(
            jax.ShapeDtypeStruct((total, 2, rows // 2, features), pool_table.dtype),
            jax.ShapeDtypeStruct((total, 1, rows), pool_items.dtype),
            jax.ShapeDtypeStruct((2,) + chosen.shape, chosen.dtype),
        ),
        scratch_shapes=[dma((3,)), dma((2,)), dma((40,)), dma, dma((total - 1,)), dma, dma((8,)), dma((8,)), dma((32,)),
                        dma((32,))],
        compiler_params=pltpu.CompilerParams(collective_id=0, has_side_effects=True),
        name="gather",
    )(pool_table.reshape(2, rows // 2, features), pool_items.reshape(1, rows), chosen)
    return table.reshape(total, rows, features), items, both


NB = 256
PB = 128


def score_kernel(chosen_s, offsets_s, place_s, hidden_ref, target_ref, labels_ref, table_ref, items_ref,
                 gh_ref, loss_ref, shares_ref, narrow_ref, slots_ref, scores, loss_acc, *, factor):
    b = pl.program_id(0)
    blocks = pl.num_programs(0)
    pair, _, kb = chosen_s.shape
    count = table_ref.shape[0]
    hists = offsets_s.shape[0] - 1
    core = place_s[1]
    base = place_s[0] + b * PB

    for other in range(pair):
        for k in range(count):
            slots_ref[other * blocks + b, k] = kb
    for other in range(pair):
        for j in range(kb):
            slots_ref[other * blocks + b, chosen_s[other, b, j]] = j

    @pl.when(b == 0)
    def _():
        loss_acc[...] = jnp.zeros_like(loss_acc)

    live = base < offsets_s[hists]
    narrow = hidden_ref[...].astype(jnp.bfloat16)
    narrow_ref[...] = narrow

    @pl.when(jnp.logical_not(live))
    def _():
        gh_ref[...] = jnp.zeros_like(gh_ref)
        shares_ref[...] = jnp.zeros_like(shares_ref)

    @pl.when(live)
    def _():
        target_wide = target_ref[...].astype(jnp.float32)
        positive = jnp.sum(narrow.astype(jnp.float32) * target_wide, axis=1, keepdims=True)
        labels = jnp.broadcast_to(labels_ref[0], (PB, PB)).T[:, :1]
        positions = base + lax.broadcasted_iota(jnp.int32, (PB, 1), 0)
        weights = jnp.zeros((PB, 1), jnp.float32)
        for h in range(hists):
            start, finish = offsets_s[h], offsets_s[h + 1]
            length = jnp.broadcast_to(finish - start, (PB, 1)).astype(jnp.float32)
            inside = (positions >= start) & (positions < finish)
            weights = weights + jnp.where(inside, 1.0 / length, 0.0)

        top = jnp.full((PB, 128), -1e30, jnp.float32)
        for j in range(kb):
            k = chosen_s[core, b, j]
            raw = lax.dot_general(narrow, table_ref[k], (((1,), (1,)), ((), ())),
                                  preferred_element_type=jnp.float32)
            masked = jnp.where(items_ref[k] == labels, -1e30, raw)
            scores[:, j * NB:(j + 1) * NB] = masked
            for i in range(NB // 128):
                top = jnp.maximum(top, masked[:, i * 128:(i + 1) * 128])
        peak = jnp.maximum(positive, jnp.max(top, axis=1, keepdims=True))
        added = jnp.zeros((PB, 128), jnp.float32)
        for j in range(kb):
            each = jnp.exp(scores[:, j * NB:(j + 1) * NB] - peak)
            scores[:, j * NB:(j + 1) * NB] = each
            for i in range(NB // 128):
                added = added + each[:, i * 128:(i + 1) * 128]
        pos_exp = jnp.exp(positive - peak)
        totals = pos_exp + jnp.sum(added, axis=1, keepdims=True)
        cross = peak + jnp.log(totals) - positive
        loss_acc[...] += jnp.broadcast_to(jnp.sum(weights * cross, axis=0, keepdims=True), loss_acc.shape)
        coeff = weights * factor
        scale = coeff / totals
        pos_grad = coeff * (pos_exp / totals - 1.0)
        out = pos_grad * target_wide
        for j in range(kb):
            k = chosen_s[core, b, j]
            g = (scores[:, j * NB:(j + 1) * NB] * scale).astype(jnp.bfloat16)
            gt = g.T
            shares_ref[0, 0, j] = gt[:128]
            shares_ref[1, 0, j] = gt[128:]
            out = out + jnp.dot(g, table_ref[k], preferred_element_type=jnp.float32)
        gh_ref[...] = out

    @pl.when(b == blocks - 1)
    def _():
        loss_ref[...] = loss_acc[...]


def score(hidden, target, labels, chosen, offsets, place, table, items, factor):
    rows, features = hidden.shape
    blocks = rows // PB
    count = table.shape[0]
    pair, _, kb = chosen.shape
    half = NB // 2
    one = pl.Buffered(1)
    grid_spec = pltpu.PrefetchScalarGridSpec(
        num_scalar_prefetch=3,
        grid=(blocks,),
        in_specs=[
            pl.BlockSpec((PB, features), lambda b, *_: (b, 0)),
            pl.BlockSpec((PB, features), lambda b, *_: (b, 0)),
            pl.BlockSpec((1, 1, PB), lambda b, *_: (b, 0, 0)),
            pl.BlockSpec((count, NB, features), lambda b, *_: (0, 0, 0), pipeline_mode=one),
            pl.BlockSpec((count, 1, NB), lambda b, *_: (0, 0, 0), pipeline_mode=one),
        ],
        out_specs=[
            pl.BlockSpec((PB, features), lambda b, *_: (b, 0)),
            pl.BlockSpec((8, 128), lambda b, *_: (0, 0)),
            pl.BlockSpec((2, 1, kb, half, PB), lambda b, *_: (0, b, 0, 0, 0)),
            pl.BlockSpec((PB, features), lambda b, *_: (b, 0)),
            pl.BlockSpec(memory_space=pltpu.SMEM),
        ],
        scratch_shapes=[
            pltpu.VMEM((PB, kb * NB), jnp.float32),
            pltpu.VMEM((8, 128), jnp.float32),
        ],
    )
    return pl.pallas_call(
        functools.partial(score_kernel, factor=factor),
        grid_spec=grid_spec,
        out_shape=(
            jax.ShapeDtypeStruct((rows, features), jnp.float32),
            jax.ShapeDtypeStruct((8, 128), jnp.float32),
            jax.ShapeDtypeStruct((2, blocks, kb, half, PB), jnp.bfloat16),
            jax.ShapeDtypeStruct((rows, features), jnp.bfloat16),
            jax.ShapeDtypeStruct((pair * blocks, count), jnp.int32),
        ),
        compiler_params=pltpu.CompilerParams(vmem_limit_bytes=60 << 20),
        name="score",
    )(chosen, offsets, place, hidden, target, labels.reshape(blocks, 1, PB), table, items)


def reduce_kernel(shares, narrow, slots, loss_in, out, loss_out, lists, wide, own, landing, landing2, landing3, parts,
                  sums, load_sem, pair_send, pair_recv, s1, r1, s2, r2, s3, r3, s4, r4, s5, r5, loss_send, loss_recv):
    x, y, z, c = where_am_i()
    partner = device(x, y, z, 1 - c)
    xs = [device(lax.rem(x + d, NX), y, z, c) for d in range(1, NX)]
    ys = [device(x, lax.rem(y + d, NY), z, c) for d in range(1, NY)]
    zs = [device(x, y, lax.rem(z + d, NZ), c) for d in range(1, NZ)]
    blocks, kb = shares.shape[1:3]
    rows = own.shape[1]
    sub = rows // NY
    length = narrow.shape[0]

    greet([partner] + xs + ys + zs)
    sent = [
        push(shares.at[1 - c], lists.at[pl.ds(c * blocks, blocks), pl.ds(0, kb)], pair_send.at[0], pair_recv.at[0], partner),
        push(narrow, wide.at[pl.ds(c * length, length)], pair_send.at[1], pair_recv.at[1], partner),
    ]
    loads = [
        pltpu.make_async_copy(shares.at[c], lists.at[pl.ds(c * blocks, blocks), pl.ds(0, kb)], load_sem.at[0]),
        pltpu.make_async_copy(narrow, wide.at[pl.ds(c * length, length)], load_sem.at[1]),
    ]
    for copy in loads:
        copy.start()
    for i in range(2 * blocks):
        lists[i, kb] = jnp.zeros(lists.shape[2:], lists.dtype)

    def loss_round(k, base, me, peers):
        parts[base + me] = sums[...]
        return [push(sums, parts.at[base + me], loss_send.at[k + d], loss_recv.at[k + d], peer)
                for d, peer in enumerate(peers)]

    def loss_sum(copies, base, count):
        for copy in copies:
            copy.wait()
        total = parts[base]
        for i in range(1, count):
            total = total + parts[base + i]
        sums[...] = total

    sums[...] = loss_in[...]
    loss_sum(loss_round(0, 0, c, [partner]), 0, 2)
    copies = loss_round(1, 2, y, ys)
    for copy in loads + sent:
        copy.wait()
    loss_sum(copies, 2, NY)
    copies = loss_round(4, 6, x, xs)

    def half(ref, h):
        size = ref.shape[0] // 2
        return ref.at[pl.ds(h * size, size)]

    def add(dst, src):
        step = 16

        @pl.loop(0, dst.shape[0] // step)
        def _(i):
            here = pl.ds(pl.multiple_of(i * step, step), step)
            dst[here] += src[here]

    def tree(n, me, subs, chunk, land, send_sems, recv_sems, up, down, before=None):
        old = {}
        for s in range(1, n // 2 + 2):
            ahead = n // 2 + 1 - s
            if before is not None:
                before(ahead)
            for j in range(subs):
                for d, to in ((1, up), (-1, down)):
                    ref = chunk(lax.rem(me + d * ahead + n, n), j)
                    if s > 1:
                        slot = ((s - 2) * subs + j) * 2 + (d < 0)
                        old[slot].wait_recv()
                        if s == 2:
                            add(half(ref, d < 0), half(land.at[slot], d < 0))
                        else:
                            add(ref, land.at[slot])
                    if ahead:
                        slot = ((s - 1) * subs + j) * 2 + (d < 0)
                        dst = land.at[slot]
                        if s == 1:
                            ref, dst = half(ref, d < 0), half(dst, d < 0)
                        old[slot] = push(ref, dst, send_sems.at[slot], recv_sems.at[slot], to)
        return list(old.values())

    group = 4

    def produce(first, count, block):
        @pl.loop(0, count)
        def _(g):
            base = (first + g) * group
            lhs = []
            for i in range(group):
                k = block(base + i)
                lhs.append(jnp.concatenate([lists[b, slots[b, k]] for b in range(2 * blocks)], axis=1))
            total = jnp.dot(jnp.concatenate(lhs, axis=0), wide[...], preferred_element_type=jnp.float32)
            for i in range(group):
                own[base + i] = total[i * rows:(i + 1) * rows]

    def run(n1, n2, me1, me2, dev, block):
        def chunk(i1, j):
            return own.at[i1 * n2 + j]

        per = n2 // group

        def before(ahead):
            if ahead == 0 or ahead == n1 // 2:
                produce(lax.rem(me1 + ahead, n1) * per, per, block)
            else:
                for d in (1, -1):
                    produce(lax.rem(me1 + d * ahead + n1, n1) * per, per, block)

        sent = tree(n1, me1, n2, chunk, landing, s1, r1, dev(lax.rem(me1 + 1, n1), me2),
                    dev(lax.rem(me1 + n1 - 1, n1), me2), before)

        def piece(i2, j):
            return own.at[me1 * n2 + i2, pl.ds(j * sub, sub)]

        sent += tree(n2, me2, NY, piece, landing2, s2, r2, dev(me1, lax.rem(me2 + 1, n2)),
                     dev(me1, lax.rem(me2 + n2 - 1, n2)))
        for copy in sent:
            copy.wait_send()

    @pl.when(c == 0)
    def _():
        run(NZ, NX, z, x, lambda i1, i2: device(i2, y, i1, 0), lambda t: (t % NX) * NZ + t // NX)

    @pl.when(c == 1)
    def _():
        run(NX, NZ, x, z, lambda i1, i2: device(i1, y, i2, 1), lambda t: t)

    loss_sum(copies, 6, NX)
    copies = loss_round(7, 10, z, zs)
    mine = own.at[(z * NX + x) * (1 - c) + (x * NZ + z) * c]
    sent = tree(NY, y, 1, lambda i, j: mine.at[pl.ds(i * sub, sub)], landing3, s3, r3, ys[0], ys[-1])

    ready = mine.at[pl.ds(y * sub, sub)]
    out[c, y] = ready[...]
    done = out.at[c, y]
    swaps = [push(ready, done, s4.at[0], r4.at[0], partner)]
    spread = [push(ready, done, s4.at[d], r4.at[d], peer) for d, peer in enumerate(ys, 1)]
    loss_sum(copies, 10, NZ)
    loss_out[...] = sums[...]
    for d, copy in enumerate(spread, 1):
        copy.wait_recv()
        ref = out.at[c, lax.rem(y + NY - d, NY)]
        swaps.append(push(ref, ref, s5.at[d - 1], r5.at[d - 1], partner))
    for copy in swaps:
        copy.wait_recv()
    for copy in sent + spread + swaps:
        copy.wait_send()


def reduce_rows(shares, narrow, slots, loss):
    pair, blocks, kb, half, width = shares.shape
    length, features = narrow.shape
    total = NX * NZ
    sub = half // NY
    dma = pltpu.SemaphoreType.DMA
    f32 = jnp.float32
    anywhere = pl.BlockSpec(memory_space=pl.ANY)
    vmem = pl.BlockSpec(memory_space=pltpu.VMEM)
    out, loss = pl.pallas_call(
        reduce_kernel,
        in_specs=[anywhere, anywhere, pl.BlockSpec(memory_space=pltpu.SMEM), vmem],
        out_specs=[vmem, vmem],
        out_shape=(jax.ShapeDtypeStruct((2, NY, sub, features), f32), jax.ShapeDtypeStruct(loss.shape, f32)),
        scratch_shapes=[
            pltpu.VMEM((pair * blocks, kb + 1, half, width), shares.dtype),
            pltpu.VMEM((pair * length, features), narrow.dtype),
            pltpu.VMEM((total, half, features), f32),
            pltpu.VMEM((32, half, features), f32),
            pltpu.VMEM((32, sub, features), f32),
            pltpu.VMEM((4, sub, features), f32),
            pltpu.VMEM((2 + NY + NX + NZ,) + loss.shape, f32),
            pltpu.VMEM(loss.shape, f32),
            dma((2,)), dma((2,)), dma((2,)),
            dma((32,)), dma((32,)), dma((32,)), dma((32,)), dma((4,)), dma((4,)),
            dma((4,)), dma((4,)), dma((3,)), dma((3,)), dma((14,)), dma((14,)),
        ],
        compiler_params=pltpu.CompilerParams(collective_id=1, has_side_effects=True, vmem_limit_bytes=56 << 20),
        name="reduce",
    )(shares, narrow, slots, loss)
    return out.reshape(2 * half, features), loss[0, 0]


def per_device(hidden, target, pool_table, pool_items, labels, chosen, offsets):
    user_count = lax.axis_size("users")
    length, features = hidden.shape[1:]
    factor = 1.0 / (user_count * (offsets.shape[1] - 1))
    table, items, both = gather(pool_table, pool_items, chosen[0])
    seq = lax.axis_index("seq")
    place = jnp.stack([seq * length, seq % 2])
    grad_hidden, loss, shares, narrow, slots = score(
        hidden[0], target[0], labels[0], both, offsets[0], place, table, items, factor
    )
    grad_table, loss_total = reduce_rows(shares, narrow, slots, loss)
    return (loss_total * factor, grad_hidden[None], grad_table)


def solution(mesh):
    return jax.shard_map(
        per_device,
        mesh=mesh,
        in_specs=(
            P("users", "seq", None),
            P("users", "seq", None),
            P("users", None),
            P("users"),
            P("users", "seq"),
            P("users", "seq", None),
            P("users", None),
        ),
        out_specs=(P(), P("users", "seq", None), P("users", None)),
        check_vma=False,
    )
```

```python
import functools
import jax
import jax.numpy as jnp
from jax import lax
from jax.experimental import pallas as pl
from jax.experimental.pallas import tpu as pltpu
from jax.sharding import PartitionSpec as P

MESH = pl.DeviceIdType.MESH
NX, NY, NZ = 4, 4, 8
EXTRA = 16


def where_am_i():
    seq, users = lax.axis_index("seq"), lax.axis_index("users")
    return users // NZ, seq // 2, users % NZ, seq % 2


def device(x, y, z, c):
    return {"seq": y * 2 + c, "users": x * NZ + z}


def greet(peers):
    barrier = pltpu.get_barrier_semaphore()
    for peer in peers:
        pl.semaphore_signal(barrier, inc=1, device_id=peer, device_id_type=MESH)
    pl.semaphore_wait(barrier, len(peers))


def push(src, dst, send_sem, recv_sem, to):
    copy = pltpu.make_async_remote_copy(src_ref=src, dst_ref=dst, send_sem=send_sem, recv_sem=recv_sem,
                                        device_id=to, device_id_type=MESH)
    copy.start()
    return copy


def gather_kernel(shard, items, chosen, table, both, whole, local_sem, pair_sem, partner_send, partner_recv, send1, recv1, send2, recv2):
    x, y, z, c = where_am_i()
    users = x * NZ + z
    total = NX * NZ
    rows = shard.shape[0]
    cut = rows * 3 // 8
    partner = device(x, y, z, 1 - c)

    whole[:rows] = shard[...]
    high = items[...] // 128
    digits = jnp.concatenate([high, items[...] - high * 128], axis=1).astype(jnp.float32)
    whole[rows:] = jnp.broadcast_to(digits, (EXTRA, digits.shape[1])).astype(whole.dtype)
    rows = rows + EXTRA

    greet([partner] + [device(lax.rem(x + d, NX), y, z, c) for d in range(1, NX)]
          + [device(x, y, lax.rem(z + d, NZ), c) for d in (1, 2, NZ - 2, NZ - 1)])
    mine = pltpu.make_async_copy(whole, table.at[users], local_sem.at[0])
    mine.start()
    mine_chosen = pltpu.make_async_copy(chosen, both.at[c], local_sem.at[1])
    mine_chosen.start()
    theirs = push(chosen, both.at[c], pair_sem.at[0], pair_sem.at[1], partner)

    def run(plan, n1, n2, me1, me2, start, count, where, dev):
        copies, pending = [], {}
        quarter = count // 2

        def region(i1, i2):
            return table.at[where(i1, i2), pl.ds(start, count)]

        def part(ref, h):
            return ref if h is None else ref.at[pl.ds(h * quarter, quarter)]

        def at(rel1, rel2):
            return region(lax.rem(me1 + rel1 + n1, n1), lax.rem(me2 + rel2 + n2, n2))

        def send(key, rel1, rel2, h, sems, to):
            dst = part(at(rel1, rel2), h)
            src = part(whole.at[pl.ds(start, count)], h) if rel1 == 0 and rel2 == 0 else dst
            pending[key] = push(src, dst, *sems, to)
            copies.append(pending[key])

        passed = []

        def arrive(key, rel1, rel2, h):
            pending.pop(key).wait_recv()
            ref = part(at(rel1, rel2), h)
            passed.append(push(ref, ref, partner_send.at[len(passed)], partner_recv, partner))

        ready = {0: 0}
        for stage, back, ahead, h in plan:
            ready[-back - ahead if abs(back + ahead) < n1 // 2 else n1 // 2] = stage
        stages = max(ready.values())
        for time in range(1, stages + n2 // 2 + 2):
            for i, (stage, back, ahead, h) in enumerate(plan):
                if stage == time - 1:
                    arrive((1, i), -back - ahead, 0, h)
            for i, (stage, back, ahead, h) in enumerate(plan):
                if stage == time:
                    send((1, i), -back, 0, h, (send1.at[i], recv1.at[i]), dev(lax.rem(me1 + ahead + n1, n1), me2))
            for sub, when in ready.items():
                s = time - when
                for d in (1, -1):
                    if 2 <= s <= n2 // 2 + 1:
                        h = None if s - 1 < n2 // 2 else int(d < 0)
                        arrive((2, sub, s - 1, d), sub, -d * (s - 1), h)
                    if 1 <= s <= n2 // 2:
                        h = None if s < n2 // 2 else int(d < 0)
                        k = ((sub % n1) * (n2 // 2) + s - 1) * 2 + (d < 0)
                        send((2, sub, s, d), sub, -d * (s - 1), h, (send2.at[k], recv2.at[k]),
                             dev(me1, lax.rem(me2 + d + n2, n2)))
        assert not pending
        for copy in copies + passed:
            copy.wait_send()
        rest = table.at[pl.ds(0, total - 1), pl.ds(0, start) if start else pl.ds(count, rows - count)]
        pltpu.make_async_copy(rest, rest, partner_recv).wait()

    across = [(1, 0, 1, None), (1, 0, -1, None), (1, 0, 2, None)]
    along = [(1, 0, 1, None), (1, 0, -1, None), (1, 0, 2, None), (1, 0, -2, None),
             (2, 2, 1, None), (2, -2, -1, None), (2, 2, 2, 0), (2, -2, -2, 1)]

    @pl.when(c == 0)
    def _():
        run(across, NX, NZ, x, z, 0, cut, lambda i1, i2: i1 * NZ + i2, lambda i1, i2: device(i1, y, i2, 0))

    @pl.when(c == 1)
    def _():
        run(along, NZ, NX, z, x, cut, rows - cut, lambda i1, i2: i2 * NZ + i1, lambda i1, i2: device(i2, y, i1, 1))

    mine.wait()
    mine_chosen.wait()
    theirs.wait()


def gather(pool_table, pool_items, chosen):
    rows, features = pool_table.shape
    total = NX * NZ
    dma = pltpu.SemaphoreType.DMA
    anywhere = pl.BlockSpec(memory_space=pl.ANY)
    table, both = pl.pallas_call(
        gather_kernel,
        in_specs=[pl.BlockSpec(memory_space=pltpu.VMEM)] * 3,
        out_specs=[anywhere] * 2,
        out_shape=(
            jax.ShapeDtypeStruct((total, rows + EXTRA, features), pool_table.dtype),
            jax.ShapeDtypeStruct((2,) + chosen.shape, chosen.dtype),
        ),
        scratch_shapes=[pltpu.VMEM((rows + EXTRA, features), pool_table.dtype),
                        dma((2,)), dma((2,)), dma((40,)), dma, dma((8,)), dma((8,)), dma((32,)),
                        dma((32,))],
        compiler_params=pltpu.CompilerParams(collective_id=0, has_side_effects=True),
        name="gather",
    )(pool_table, pool_items.reshape(1, rows), chosen)
    return table, both


NB = 256
PB = 128


def score_kernel(chosen_s, offsets_s, hidden_ref, target_ref, labels_ref, table_ref,
                 gh_ref, loss_ref, shares_ref, narrow_ref, slots_ref, scores, loss_acc, *, factor):
    b = pl.program_id(0)
    blocks = pl.num_programs(0)
    pair, _, kb = chosen_s.shape
    count = table_ref.shape[0]
    hists = offsets_s.shape[0] - 1
    seq = lax.axis_index("seq")
    core = seq % 2
    base = (seq * blocks + b) * PB

    for other in range(pair):
        for k in range(count):
            slots_ref[other * blocks + b, k] = kb
    for other in range(pair):
        for j in range(kb):
            slots_ref[other * blocks + b, chosen_s[other, b, j]] = j

    @pl.when(b == 0)
    def _():
        loss_acc[...] = jnp.zeros_like(loss_acc)

    live = base < offsets_s[hists]
    narrow = hidden_ref[...].astype(jnp.bfloat16)
    narrow_ref[...] = narrow

    @pl.when(jnp.logical_not(live))
    def _():
        gh_ref[...] = jnp.zeros_like(gh_ref)
        shares_ref[...] = jnp.zeros_like(shares_ref)

    @pl.when(live)
    def _():
        target_wide = target_ref[...].astype(jnp.float32)
        positive = jnp.sum(narrow.astype(jnp.float32) * target_wide, axis=1, keepdims=True)
        labels = jnp.broadcast_to(labels_ref[0].astype(jnp.float32), (PB, PB)).T[:, :1]
        positions = base + lax.broadcasted_iota(jnp.int32, (PB, 1), 0)
        weights = jnp.zeros((PB, 1), jnp.float32)
        for h in range(hists):
            start, finish = offsets_s[h], offsets_s[h + 1]
            length = jnp.broadcast_to(finish - start, (PB, 1)).astype(jnp.float32)
            inside = (positions >= start) & (positions < finish)
            weights = weights + jnp.where(inside, 1.0 / length, 0.0)

        top = jnp.full((PB, 128), -1e30, jnp.float32)
        for j in range(kb):
            k = chosen_s[core, b, j]
            rows = table_ref[k, :NB]
            digits = table_ref[k, NB:][:1].astype(jnp.float32)
            items = digits[:, :NB] * 128.0 + digits[:, NB:]
            raw = lax.dot_general(narrow, rows, (((1,), (1,)), ((), ())),
                                  preferred_element_type=jnp.float32)
            masked = jnp.where(items == labels, -1e30, raw)
            scores[:, j * NB:(j + 1) * NB] = masked
            for i in range(NB // 128):
                top = jnp.maximum(top, masked[:, i * 128:(i + 1) * 128])
        peak = jnp.maximum(positive, jnp.max(top, axis=1, keepdims=True))
        added = jnp.zeros((PB, 128), jnp.float32)
        for j in range(kb):
            each = jnp.exp(scores[:, j * NB:(j + 1) * NB] - peak)
            scores[:, j * NB:(j + 1) * NB] = each
            for i in range(NB // 128):
                added = added + each[:, i * 128:(i + 1) * 128]
        pos_exp = jnp.exp(positive - peak)
        totals = pos_exp + jnp.sum(added, axis=1, keepdims=True)
        cross = peak + jnp.log(totals) - positive
        loss_acc[...] += jnp.broadcast_to(jnp.sum(weights * cross, axis=0, keepdims=True), loss_acc.shape)
        coeff = weights * factor
        scale = coeff / totals
        pos_grad = coeff * (pos_exp / totals - 1.0)
        out = pos_grad * target_wide
        for j in range(kb):
            k = chosen_s[core, b, j]
            g = (scores[:, j * NB:(j + 1) * NB] * scale).astype(jnp.bfloat16)
            gt = g.T
            shares_ref[0, 0, j] = gt[:128]
            shares_ref[1, 0, j] = gt[128:]
            out = out + jnp.dot(g, table_ref[k, :NB], preferred_element_type=jnp.float32)
        gh_ref[...] = out

    @pl.when(b == blocks - 1)
    def _():
        loss_ref[...] = loss_acc[...] * factor


def score(hidden, target, labels, chosen, offsets, table, factor):
    rows, features = hidden.shape
    blocks = rows // PB
    count = table.shape[0]
    pair, _, kb = chosen.shape
    half = NB // 2
    one = pl.Buffered(1)
    grid_spec = pltpu.PrefetchScalarGridSpec(
        num_scalar_prefetch=2,
        grid=(blocks,),
        in_specs=[
            pl.BlockSpec((PB, features), lambda b, *_: (b, 0)),
            pl.BlockSpec((PB, features), lambda b, *_: (b, 0)),
            pl.BlockSpec((1, 1, PB), lambda b, *_: (b, 0, 0)),
            pl.BlockSpec(table.shape, lambda b, *_: (0, 0, 0), pipeline_mode=one),
        ],
        out_specs=[
            pl.BlockSpec((PB, features), lambda b, *_: (b, 0)),
            pl.BlockSpec((8, 128), lambda b, *_: (0, 0)),
            pl.BlockSpec((2, 1, kb, half, PB), lambda b, *_: (0, b, 0, 0, 0)),
            pl.BlockSpec((PB, features), lambda b, *_: (b, 0)),
            pl.BlockSpec(memory_space=pltpu.SMEM),
        ],
        scratch_shapes=[
            pltpu.VMEM((PB, kb * NB), jnp.float32),
            pltpu.VMEM((8, 128), jnp.float32),
        ],
    )
    return pl.pallas_call(
        functools.partial(score_kernel, factor=factor),
        grid_spec=grid_spec,
        out_shape=(
            jax.ShapeDtypeStruct((rows, features), jnp.float32),
            jax.ShapeDtypeStruct((8, 128), jnp.float32),
            jax.ShapeDtypeStruct((2, blocks, kb, half, PB), jnp.bfloat16),
            jax.ShapeDtypeStruct((rows, features), jnp.bfloat16),
            jax.ShapeDtypeStruct((pair * blocks, count), jnp.int32),
        ),
        compiler_params=pltpu.CompilerParams(vmem_limit_bytes=60 << 20),
        name="score",
    )(chosen, offsets, hidden, target, labels.reshape(blocks, 1, PB), table)


MAIN = 384


def reduce_kernel(shares, narrow, slots, loss_in, out, loss_out, lists, wide, own, side, ready, landing, landing2,
                  landing3, landing4, landing5, parts, sums, load_sem, pair_send, pair_recv, s1, r1, s2, r2, s3, r3,
                  s4, r4, s5, r5, s6, r6, s7, r7, loss_send, loss_recv):
    x, y, z, c = where_am_i()
    users = x * NZ + z
    total = NX * NZ
    partner = device(x, y, z, 1 - c)
    xs = [device(lax.rem(x + d, NX), y, z, c) for d in range(1, NX)]
    ys = [device(x, lax.rem(y + d, NY), z, c) for d in range(1, NY)]
    zs = [device(x, y, lax.rem(z + d, NZ), c) for d in range(1, NZ)]
    others = [lax.rem(users + d, total) for d in range(1, total)]
    plane = [{"seq": y * 2 + c, "users": u} for u in others]
    blocks, kb = shares.shape[1:3]
    rows = own.shape[1]
    sub = rows // NY
    length = narrow.shape[0]

    def loss_round(k, base, me, peers):
        parts[base + me] = sums[...]
        return [push(sums, parts.at[base + me], loss_send.at[k + d], loss_recv.at[k + d], peer)
                for d, peer in enumerate(peers)]

    def loss_sum(copies, base, count):
        for copy in copies:
            copy.wait()
        added = parts[base]
        for i in range(1, count):
            added = added + parts[base + i]
        sums[...] = added

    sums[...] = loss_in[...]
    greet([partner] + ys + plane)
    losses = loss_round(0, 0, c, [partner])
    pair = [
        push(shares.at[1 - c], lists.at[pl.ds(c * blocks, blocks), pl.ds(0, kb)], pair_send.at[0], pair_recv.at[0], partner),
        push(narrow, wide.at[pl.ds(c * length, length)], pair_send.at[1], pair_recv.at[1], partner),
        pltpu.make_async_copy(shares.at[c], lists.at[pl.ds(c * blocks, blocks), pl.ds(0, kb)], load_sem.at[0]),
        pltpu.make_async_copy(narrow, wide.at[pl.ds(c * length, length)], load_sem.at[1]),
    ]
    for copy in pair[2:]:
        copy.start()
    for i in range(2 * blocks):
        lists[i, kb] = jnp.zeros(lists.shape[2:], lists.dtype)
    loss_sum(losses, 0, 2)
    for copy in pair:
        copy.wait()

    def half(ref, h):
        size = ref.shape[0] // 2
        return ref.at[pl.ds(h * size, size)]

    def add(dst, src):
        step = min(dst.shape[0], 64 if len(dst.shape) == 2 else 4)

        @pl.loop(0, dst.shape[0] // step)
        def _(i):
            here = pl.ds(pl.multiple_of(i * step, step), step)
            dst[here] += src[here]

    def tree(n, me, order, chunk, land, send_sems, recv_sems, up, down, fine=False):
        old = {}
        subs = len(order)
        for s in range(1, n // 2 + 2):
            ahead = n // 2 + 1 - s
            for i, j in enumerate(order):
                for d, to in ((1, up), (-1, down)):
                    ref = chunk(lax.rem(me + d * ahead + n, n), j)
                    if s > 1:
                        slot = ((s - 2) * subs + i) * 2 + (d < 0)
                        old[slot].wait_recv()
                        if s == 2:
                            add(half(ref, d < 0), half(land.at[slot], d < 0))
                        else:
                            add(ref, land.at[slot])
                    if ahead:
                        slot = ((s - 1) * subs + i) * 2 + (d < 0)
                        dst = land.at[slot]
                        if s == 1:
                            ref, dst = half(ref, d < 0), half(dst, d < 0)
                        old[slot] = push(ref, dst, send_sems.at[slot], recv_sems.at[slot], to)
                if fine and not ahead:
                    yield list(old.values())
            if ahead or not fine:
                yield list(old.values())

    def finish(steps):
        for copies in steps:
            pass
        return copies

    group = 4

    def produce(first, count, block):
        @pl.loop(0, count)
        def _(g):
            base = (first + g) * group
            lhs = []
            for i in range(group):
                k = block(base + i)
                lhs.append(jnp.concatenate([lists[b, slots[b, k]] for b in range(2 * blocks)], axis=1))
            found = jnp.dot(jnp.concatenate(lhs, axis=0), wide[...], preferred_element_type=jnp.float32)
            for i in range(group):
                own[base + i] = found[i * rows:(i + 1) * rows, :MAIN]
                for w in range(NY):
                    side[w, block(base + i)] = found[i * rows + w * sub:i * rows + (w + 1) * sub, MAIN:]

    def run(n1, n2, me1, me2, dev, block):
        per = n2 // group

        def make(*places):
            for place in places:
                produce(lax.rem(me1 + place + n1, n1) * per, per, block)

        reach = [n2 // 2] + [r for q in range(n2 // 2 - 1, 0, -1) for r in (q, -q)] + [0]
        main = tree(n1, me1, [lax.rem(me2 + r + n2, n2) for r in reach], lambda i1, j: own.at[i1 * n2 + j], landing,
                    s1, r1, dev(lax.rem(me1 + 1, n1), me2), dev(lax.rem(me1 + n1 - 1, n1), me2), fine=True)
        edge = tree(NY, y, range(NX), lambda i, j: side.at[i, pl.ds(j * NZ, NZ)], landing4, s6, r6, ys[0], ys[-1])
        second = tree(n2, me2, range(NY), lambda i, j: own.at[me1 * n2 + i, pl.ds(j * sub, sub)], landing2, s2, r2,
                      dev(me1, lax.rem(me2 + 1, n2)), dev(me1, lax.rem(me2 + n2 - 1, n2)))
        mine = own.at[me1 * n2 + me2]
        last = tree(NY, y, [0], lambda i, j: mine.at[pl.ds(i * sub, sub)], landing3, s3, r3, ys[0], ys[-1])
        make(n1 // 2)
        next(main)
        losses = loss_round(1, 2, y, ys)
        if n1 == NZ:
            make(3, -3)
            next(main)
            make(2, -2)
        make(1, -1, 0)
        next(edge)
        next(main)
        loss_sum(losses, 2, NY)
        losses = loss_round(4, 6, x, xs)
        next(edge)
        if n1 == NZ:
            next(main)
        sent = next(main)
        next(second)
        for _ in range(n2 // 2 - 1):
            next(main)
            next(main)
            next(second)
        next(main)
        loss_sum(losses, 6, NX)
        losses = loss_round(7, 10, z, zs)
        sent += finish(edge)
        direct = [push(side.at[y, u], landing5.at[d], s7.at[d], r7.at[d], peer)
                  for d, (u, peer) in enumerate(zip(others, plane))]
        sent += finish(second)
        sent += finish(last)
        ready[:, :MAIN] = mine[pl.ds(y * sub, sub)]
        for copy in direct:
            copy.wait_recv()
        found = side[y, users]
        for d in range(total - 1):
            found = found + landing5[d]
        ready[:, MAIN:] = found
        loss_sum(losses, 10, NZ)
        for copy in sent + direct:
            copy.wait_send()

    @pl.when(c == 0)
    def _():
        run(NZ, NX, z, x, lambda i1, i2: device(i2, y, i1, 0), lambda t: (t % NX) * NZ + t // NX)

    @pl.when(c == 1)
    def _():
        run(NX, NZ, x, z, lambda i1, i2: device(i1, y, i2, 1), lambda t: t)

    done = out.at[c, y]
    swaps = [push(ready, done, s4.at[0], r4.at[0], partner)]
    spread = [push(ready, done, s4.at[d], r4.at[d], peer) for d, peer in enumerate(ys, 1)]
    out[c, y] = ready[...]
    loss_out[...] = sums[:1, :1]
    for d, copy in enumerate(spread, 1):
        copy.wait_recv()
        ref = out.at[c, lax.rem(y + NY - d, NY)]
        swaps.append(push(ref, ref, s5.at[d - 1], r5.at[d - 1], partner))
    for copy in swaps:
        copy.wait_recv()
    for copy in spread + swaps:
        copy.wait_send()


def reduce_rows(shares, narrow, slots, loss):
    pair, blocks, kb, half, width = shares.shape
    length, features = narrow.shape
    total = NX * NZ
    sub = half // NY
    edge = features - MAIN
    dma = pltpu.SemaphoreType.DMA
    f32 = jnp.float32
    anywhere = pl.BlockSpec(memory_space=pl.ANY)
    vmem = pl.BlockSpec(memory_space=pltpu.VMEM)
    out, loss = pl.pallas_call(
        reduce_kernel,
        in_specs=[anywhere, anywhere, pl.BlockSpec(memory_space=pltpu.SMEM), vmem],
        out_specs=[vmem, vmem],
        out_shape=(jax.ShapeDtypeStruct((2, NY, sub, features), f32), jax.ShapeDtypeStruct((1, 1), f32)),
        scratch_shapes=[
            pltpu.VMEM((pair * blocks, kb + 1, half, width), shares.dtype),
            pltpu.VMEM((pair * length, features), narrow.dtype),
            pltpu.VMEM((total, half, MAIN), f32),
            pltpu.VMEM((NY, total, sub, edge), f32),
            pltpu.VMEM((sub, features), f32),
            pltpu.VMEM((32, half, MAIN), f32),
            pltpu.VMEM((32, sub, MAIN), f32),
            pltpu.VMEM((4, sub, MAIN), f32),
            pltpu.VMEM((16, NZ, sub, edge), f32),
            pltpu.VMEM((total - 1, sub, edge), f32),
            pltpu.VMEM((2 + NY + NX + NZ,) + loss.shape, f32),
            pltpu.VMEM(loss.shape, f32),
            dma((2,)), dma((2,)), dma((2,)),
            dma((32,)), dma((32,)), dma((32,)), dma((32,)), dma((4,)), dma((4,)),
            dma((4,)), dma((4,)), dma((3,)), dma((3,)), dma((16,)), dma((16,)), dma((total - 1,)), dma((total - 1,)),
            dma((14,)), dma((14,)),
        ],
        compiler_params=pltpu.CompilerParams(collective_id=1, has_side_effects=True, vmem_limit_bytes=63 << 20),
        name="reduce",
    )(shares, narrow, slots, loss)
    return out.reshape(2 * half, features), loss.reshape(())


def per_device(hidden, target, pool_table, pool_items, labels, chosen, offsets):
    user_count = lax.axis_size("users")
    factor = 1.0 / (user_count * (offsets.shape[1] - 1))
    table, both = gather(pool_table, pool_items, chosen[0])
    grad_hidden, loss, shares, narrow, slots = score(
        hidden[0], target[0], labels[0], both, offsets[0], table, factor
    )
    grad_table, loss_total = reduce_rows(shares, narrow, slots, loss)
    return (loss_total, grad_hidden[None], grad_table)


def solution(mesh):
    return jax.shard_map(
        per_device,
        mesh=mesh,
        in_specs=(
            P("users", "seq", None),
            P("users", "seq", None),
            P("users", None),
            P("users"),
            P("users", "seq"),
            P("users", "seq", None),
            P("users", None),
        ),
        out_specs=(P(), P("users", "seq", None), P("users", None)),
        check_vma=False,
    )
```

```python
import functools
import jax
import jax.numpy as jnp
from jax import lax
from jax.experimental import pallas as pl
from jax.experimental.pallas import tpu as pltpu
from jax.sharding import PartitionSpec as P

MESH = pl.DeviceIdType.MESH
NX, NY, NZ = 4, 4, 8
EXTRA = 16


def where_am_i():
    seq, users = lax.axis_index("seq"), lax.axis_index("users")
    return users // NZ, seq // 2, users % NZ, seq % 2


def device(x, y, z, c):
    return {"seq": y * 2 + c, "users": x * NZ + z}


def greet(peers):
    barrier = pltpu.get_barrier_semaphore()
    for peer in peers:
        pl.semaphore_signal(barrier, inc=1, device_id=peer, device_id_type=MESH)
    pl.semaphore_wait(barrier, len(peers))


def push(src, dst, send_sem, recv_sem, to):
    copy = pltpu.make_async_remote_copy(src_ref=src, dst_ref=dst, send_sem=send_sem, recv_sem=recv_sem,
                                        device_id=to, device_id_type=MESH)
    copy.start()
    return copy


def gather_kernel(shard, items, chosen, table, both, whole, local_sem, pair_sem, partner_send, partner_recv, send1, recv1, send2, recv2):
    x, y, z, c = where_am_i()
    users = x * NZ + z
    total = NX * NZ
    rows = shard.shape[0]
    cut = rows * 3 // 8
    partner = device(x, y, z, 1 - c)

    whole[:rows] = shard[...]
    high = items[...] // 128
    digits = jnp.concatenate([high, items[...] - high * 128], axis=1).astype(jnp.float32)
    whole[rows:] = jnp.broadcast_to(digits, (EXTRA, digits.shape[1])).astype(whole.dtype)
    rows = rows + EXTRA

    greet([partner] + [device(lax.rem(x + d, NX), y, z, c) for d in range(1, NX)]
          + [device(x, y, lax.rem(z + d, NZ), c) for d in (1, 2, NZ - 2, NZ - 1)])
    mine = pltpu.make_async_copy(whole, table.at[users], local_sem.at[0])
    mine.start()
    mine_chosen = pltpu.make_async_copy(chosen, both.at[c], local_sem.at[1])
    mine_chosen.start()
    theirs = push(chosen, both.at[c], pair_sem.at[0], pair_sem.at[1], partner)

    def run(plan, n1, n2, me1, me2, start, count, where, dev):
        copies, pending = [], {}
        quarter = count // 2

        def region(i1, i2):
            return table.at[where(i1, i2), pl.ds(start, count)]

        def part(ref, h):
            return ref if h is None else ref.at[pl.ds(h * quarter, quarter)]

        def at(rel1, rel2):
            return region(lax.rem(me1 + rel1 + n1, n1), lax.rem(me2 + rel2 + n2, n2))

        def send(key, rel1, rel2, h, sems, to):
            dst = part(at(rel1, rel2), h)
            src = part(whole.at[pl.ds(start, count)], h) if rel1 == 0 and rel2 == 0 else dst
            pending[key] = push(src, dst, *sems, to)
            copies.append(pending[key])

        passed = []

        def arrive(key, rel1, rel2, h):
            pending.pop(key).wait_recv()
            ref = part(at(rel1, rel2), h)
            passed.append(push(ref, ref, partner_send.at[len(passed)], partner_recv, partner))

        ready = {0: 0}
        for stage, back, ahead, h in plan:
            ready[-back - ahead if abs(back + ahead) < n1 // 2 else n1 // 2] = stage
        stages = max(ready.values())
        for time in range(1, stages + n2 // 2 + 2):
            for i, (stage, back, ahead, h) in enumerate(plan):
                if stage == time - 1:
                    arrive((1, i), -back - ahead, 0, h)
            for i, (stage, back, ahead, h) in enumerate(plan):
                if stage == time:
                    send((1, i), -back, 0, h, (send1.at[i], recv1.at[i]), dev(lax.rem(me1 + ahead + n1, n1), me2))
            for sub, when in ready.items():
                s = time - when
                for d in (1, -1):
                    if 2 <= s <= n2 // 2 + 1:
                        h = None if s - 1 < n2 // 2 else int(d < 0)
                        arrive((2, sub, s - 1, d), sub, -d * (s - 1), h)
                    if 1 <= s <= n2 // 2:
                        h = None if s < n2 // 2 else int(d < 0)
                        k = ((sub % n1) * (n2 // 2) + s - 1) * 2 + (d < 0)
                        send((2, sub, s, d), sub, -d * (s - 1), h, (send2.at[k], recv2.at[k]),
                             dev(me1, lax.rem(me2 + d + n2, n2)))
        assert not pending
        for copy in copies + passed:
            copy.wait_send()
        rest = table.at[pl.ds(0, total - 1), pl.ds(0, start) if start else pl.ds(count, rows - count)]
        pltpu.make_async_copy(rest, rest, partner_recv).wait()

    across = [(1, 0, 1, None), (1, 0, -1, None), (1, 0, 2, None)]
    along = [(1, 0, 1, None), (1, 0, -1, None), (1, 0, 2, None), (1, 0, -2, None),
             (2, 2, 1, None), (2, -2, -1, None), (2, 2, 2, 0), (2, -2, -2, 1)]

    @pl.when(c == 0)
    def _():
        run(across, NX, NZ, x, z, 0, cut, lambda i1, i2: i1 * NZ + i2, lambda i1, i2: device(i1, y, i2, 0))

    @pl.when(c == 1)
    def _():
        run(along, NZ, NX, z, x, cut, rows - cut, lambda i1, i2: i2 * NZ + i1, lambda i1, i2: device(i2, y, i1, 1))

    mine.wait()
    mine_chosen.wait()
    theirs.wait()


def gather(pool_table, pool_items, chosen):
    rows, features = pool_table.shape
    total = NX * NZ
    dma = pltpu.SemaphoreType.DMA
    anywhere = pl.BlockSpec(memory_space=pl.ANY)
    table, both = pl.pallas_call(
        gather_kernel,
        in_specs=[pl.BlockSpec(memory_space=pltpu.VMEM)] * 3,
        out_specs=[anywhere] * 2,
        out_shape=(
            jax.ShapeDtypeStruct((total, rows + EXTRA, features), pool_table.dtype),
            jax.ShapeDtypeStruct((2,) + chosen.shape, chosen.dtype),
        ),
        scratch_shapes=[pltpu.VMEM((rows + EXTRA, features), pool_table.dtype),
                        dma((2,)), dma((2,)), dma((40,)), dma, dma((8,)), dma((8,)), dma((32,)),
                        dma((32,))],
        compiler_params=pltpu.CompilerParams(collective_id=0, has_side_effects=True),
        name="gather",
    )(pool_table, pool_items.reshape(1, rows), chosen)
    return table, both


NB = 256
PB = 128
TOGETHER = 2


def score_kernel(chosen_s, offsets_s, hidden_ref, target_ref, labels_ref, table_ref,
                 gh_ref, loss_ref, shares_ref, narrow_ref, slots_ref, scores, loss_acc, *, factor):
    step = pl.program_id(0)
    steps = pl.num_programs(0)
    pair, blocks, kb = chosen_s.shape
    count = table_ref.shape[0]
    hists = offsets_s.shape[0] - 1
    seq = lax.axis_index("seq")
    core = seq % 2

    for u in range(TOGETHER):
        b = step * TOGETHER + u
        for other in range(pair):
            for k in range(count):
                slots_ref[other * blocks + b, k] = kb
        for other in range(pair):
            for j in range(kb):
                slots_ref[other * blocks + b, chosen_s[other, b, j]] = j

    @pl.when(step == 0)
    def _():
        loss_acc[...] = jnp.zeros_like(loss_acc)

    first = (seq * blocks + step * TOGETHER) * PB
    live = first < offsets_s[hists]
    narrow_ref[...] = hidden_ref[...].astype(jnp.bfloat16)

    @pl.when(jnp.logical_not(live))
    def _():
        gh_ref[...] = jnp.zeros_like(gh_ref)
        shares_ref[...] = jnp.zeros_like(shares_ref)

    def look(u):
        b = step * TOGETHER + u
        rows = pl.ds(u * PB, PB)
        narrow = hidden_ref[rows].astype(jnp.bfloat16)
        positive = jnp.sum(narrow.astype(jnp.float32) * target_ref[rows].astype(jnp.float32), axis=1, keepdims=True)
        labels = jnp.broadcast_to(labels_ref[u].astype(jnp.float32), (PB, PB)).T[:, :1]
        top = jnp.full((PB, 128), -1e30, jnp.float32)
        for j in range(kb):
            k = chosen_s[core, b, j]
            digits = table_ref[k, NB:][:1].astype(jnp.float32)
            items = digits[:, :NB] * 128.0 + digits[:, NB:]
            raw = lax.dot_general(narrow, table_ref[k, :NB], (((1,), (1,)), ((), ())),
                                  preferred_element_type=jnp.float32)
            masked = jnp.where(items == labels, -1e30, raw)
            scores[u, :, j * NB:(j + 1) * NB] = masked
            for i in range(NB // 128):
                top = jnp.maximum(top, masked[:, i * 128:(i + 1) * 128])
        return positive, jnp.maximum(positive, jnp.max(top, axis=1, keepdims=True))

    def weigh(u, positive, peak):
        positions = first + u * PB + lax.broadcasted_iota(jnp.int32, (PB, 1), 0)
        weights = jnp.zeros((PB, 1), jnp.float32)
        for h in range(hists):
            start, finish = offsets_s[h], offsets_s[h + 1]
            length = jnp.broadcast_to(finish - start, (PB, 1)).astype(jnp.float32)
            inside = (positions >= start) & (positions < finish)
            weights = weights + jnp.where(inside, 1.0 / length, 0.0)
        added = jnp.zeros((PB, 128), jnp.float32)
        for j in range(kb):
            each = jnp.exp(scores[u, :, j * NB:(j + 1) * NB] - peak)
            scores[u, :, j * NB:(j + 1) * NB] = each
            for i in range(NB // 128):
                added = added + each[:, i * 128:(i + 1) * 128]
        pos_exp = jnp.exp(positive - peak)
        totals = pos_exp + jnp.sum(added, axis=1, keepdims=True)
        cross = peak + jnp.log(totals) - positive
        loss_acc[...] += jnp.broadcast_to(jnp.sum(weights * cross, axis=0, keepdims=True), loss_acc.shape)
        coeff = weights * factor
        return coeff / totals, coeff * (pos_exp / totals - 1.0)

    def pull(u, scale, pos_grad):
        b = step * TOGETHER + u
        rows = pl.ds(u * PB, PB)
        out = pos_grad * target_ref[rows].astype(jnp.float32)
        for j in range(kb):
            k = chosen_s[core, b, j]
            g = (scores[u, :, j * NB:(j + 1) * NB] * scale).astype(jnp.bfloat16)
            gt = g.T
            shares_ref[0, u, j] = gt[:PB]
            shares_ref[1, u, j] = gt[PB:]
            out = out + jnp.dot(g, table_ref[k, :NB], preferred_element_type=jnp.float32)
        gh_ref[rows] = out

    @pl.when(live)
    def _():
        seen = [look(0)]
        for u in range(TOGETHER):
            if u + 1 < TOGETHER:
                seen.append(look(u + 1))
            pull(u, *weigh(u, *seen[u]))

    @pl.when(step == steps - 1)
    def _():
        loss_ref[...] = loss_acc[...] * factor


def score(hidden, target, labels, chosen, offsets, table, factor):
    rows, features = hidden.shape
    blocks = rows // PB
    count = table.shape[0]
    pair, _, kb = chosen.shape
    half = NB // 2
    one = pl.Buffered(1)
    grid_spec = pltpu.PrefetchScalarGridSpec(
        num_scalar_prefetch=2,
        grid=(blocks // TOGETHER,),
        in_specs=[
            pl.BlockSpec((TOGETHER * PB, features), lambda b, *_: (b, 0)),
            pl.BlockSpec((TOGETHER * PB, features), lambda b, *_: (b, 0)),
            pl.BlockSpec((TOGETHER, 1, PB), lambda b, *_: (b, 0, 0)),
            pl.BlockSpec(table.shape, lambda b, *_: (0, 0, 0), pipeline_mode=one),
        ],
        out_specs=[
            pl.BlockSpec((TOGETHER * PB, features), lambda b, *_: (b, 0)),
            pl.BlockSpec((8, 128), lambda b, *_: (0, 0)),
            pl.BlockSpec((2, TOGETHER, kb, half, PB), lambda b, *_: (0, b, 0, 0, 0)),
            pl.BlockSpec((TOGETHER * PB, features), lambda b, *_: (b, 0)),
            pl.BlockSpec(memory_space=pltpu.SMEM),
        ],
        scratch_shapes=[
            pltpu.VMEM((TOGETHER, PB, kb * NB), jnp.float32),
            pltpu.VMEM((8, 128), jnp.float32),
        ],
    )
    return pl.pallas_call(
        functools.partial(score_kernel, factor=factor),
        grid_spec=grid_spec,
        out_shape=(
            jax.ShapeDtypeStruct((rows, features), jnp.float32),
            jax.ShapeDtypeStruct((8, 128), jnp.float32),
            jax.ShapeDtypeStruct((2, blocks, kb, half, PB), jnp.bfloat16),
            jax.ShapeDtypeStruct((rows, features), jnp.bfloat16),
            jax.ShapeDtypeStruct((pair * blocks, count), jnp.int32),
        ),
        compiler_params=pltpu.CompilerParams(vmem_limit_bytes=60 << 20),
        name="score",
    )(chosen, offsets, hidden, target, labels.reshape(blocks, 1, PB), table)


MAIN = 384


def reduce_kernel(shares, narrow, slots, loss_in, out, loss_out, lists, wide, own, side, ready, last, landing, landing2,
                  landing3, landing4, landing5, parts, sums, load_sem, pair_send, pair_recv, s1, r1, s2, r2, s3, r3,
                  s4, r4, s5, r5, s6, r6, s7, r7, loss_send, loss_recv):
    x, y, z, c = where_am_i()
    users = x * NZ + z
    total = NX * NZ
    partner = device(x, y, z, 1 - c)
    xs = [device(lax.rem(x + d, NX), y, z, c) for d in range(1, NX)]
    ys = [device(x, lax.rem(y + d, NY), z, c) for d in range(1, NY)]
    zs = [device(x, y, lax.rem(z + d, NZ), c) for d in range(1, NZ)]
    others = [lax.rem(users + d, total) for d in range(1, total)]
    plane = [{"seq": y * 2 + c, "users": u} for u in others]
    blocks, kb = shares.shape[1:3]
    rows = own.shape[1]
    sub = rows // NY
    length = narrow.shape[0]

    def loss_round(k, base, me, peers):
        parts[base + me] = sums[...]
        return [push(sums, parts.at[base + me], loss_send.at[k + d], loss_recv.at[k + d], peer)
                for d, peer in enumerate(peers)]

    def loss_sum(copies, base, count):
        for copy in copies:
            copy.wait()
        added = parts[base]
        for i in range(1, count):
            added = added + parts[base + i]
        sums[...] = added

    sums[...] = loss_in[...]
    greet([partner] + ys + plane)
    losses = loss_round(0, 0, c, [partner])
    pair = [
        push(shares.at[1 - c], lists.at[pl.ds(c * blocks, blocks), pl.ds(0, kb)], pair_send.at[0], pair_recv.at[0], partner),
        push(narrow, wide.at[pl.ds(c * length, length)], pair_send.at[1], pair_recv.at[1], partner),
        pltpu.make_async_copy(shares.at[c], lists.at[pl.ds(c * blocks, blocks), pl.ds(0, kb)], load_sem.at[0]),
        pltpu.make_async_copy(narrow, wide.at[pl.ds(c * length, length)], load_sem.at[1]),
    ]
    for copy in pair[2:]:
        copy.start()
    for i in range(2 * blocks):
        lists[i, kb] = jnp.zeros(lists.shape[2:], lists.dtype)
    loss_sum(losses, 0, 2)
    for copy in pair:
        copy.wait()

    def half(ref, h):
        size = ref.shape[0] // 2
        return ref.at[pl.ds(h * size, size)]

    def add(dst, src):
        step = min(dst.shape[0], 64 if len(dst.shape) == 2 else 4)

        @pl.loop(0, dst.shape[0] // step)
        def _(i):
            here = pl.ds(pl.multiple_of(i * step, step), step)
            dst[here] += src[here]

    def tree(n, me, order, chunk, land, send_sems, recv_sems, up, down, fine=False):
        old = {}
        subs = len(order)
        for s in range(1, n // 2 + 2):
            ahead = n // 2 + 1 - s
            for i, j in enumerate(order):
                for d, to in ((1, up), (-1, down)):
                    ref = chunk(lax.rem(me + d * ahead + n, n), j)
                    if s > 1:
                        slot = ((s - 2) * subs + i) * 2 + (d < 0)
                        old[slot].wait_recv()
                        if s == 2:
                            add(half(ref, d < 0), half(land.at[slot], d < 0))
                        else:
                            add(ref, land.at[slot])
                    if ahead:
                        slot = ((s - 1) * subs + i) * 2 + (d < 0)
                        dst = land.at[slot]
                        if s == 1:
                            ref, dst = half(ref, d < 0), half(dst, d < 0)
                        old[slot] = push(ref, dst, send_sems.at[slot], recv_sems.at[slot], to)
                if fine and not ahead:
                    yield list(old.values())
            if ahead or not fine:
                yield list(old.values())

    def finish(steps):
        for copies in steps:
            pass
        return copies

    def share(ref, start, width, base):
        done = out.at[c, y, :, pl.ds(start, width)]
        return [push(ref, done, s4.at[base + d], r4.at[base + d], peer) for d, peer in enumerate([partner] + ys)]

    group = 4

    def produce(first, count, block):
        @pl.loop(0, count)
        def _(g):
            base = (first + g) * group
            lhs = []
            for i in range(group):
                k = block(base + i)
                lhs.append(jnp.concatenate([lists[b, slots[b, k]] for b in range(2 * blocks)], axis=1))
            found = jnp.dot(jnp.concatenate(lhs, axis=0), wide[...], preferred_element_type=jnp.float32)
            for i in range(group):
                own[base + i] = found[i * rows:(i + 1) * rows, :MAIN]
                for w in range(NY):
                    side[w, block(base + i)] = found[i * rows + w * sub:i * rows + (w + 1) * sub, MAIN:]

    def run(n1, n2, me1, me2, dev, block):
        per = n2 // group

        def make(*places):
            for place in places:
                produce(lax.rem(me1 + place + n1, n1) * per, per, block)

        reach = [n2 // 2] + [r for q in range(n2 // 2 - 1, 0, -1) for r in (q, -q)] + [0]
        main = tree(n1, me1, [lax.rem(me2 + r + n2, n2) for r in reach], lambda i1, j: own.at[i1 * n2 + j], landing,
                    s1, r1, dev(lax.rem(me1 + 1, n1), me2), dev(lax.rem(me1 + n1 - 1, n1), me2), fine=True)
        edge = tree(NY, y, range(NX), lambda i, j: side.at[i, pl.ds(j * NZ, NZ)], landing4, s6, r6, ys[0], ys[-1])
        second = tree(n2, me2, range(NY), lambda i, j: own.at[me1 * n2 + i, pl.ds(j * sub, sub)], landing2, s2, r2,
                      dev(me1, lax.rem(me2 + 1, n2)), dev(me1, lax.rem(me2 + n2 - 1, n2)))
        mine = own.at[me1 * n2 + me2]
        make(n1 // 2)
        next(main)
        losses = loss_round(1, 2, y, ys)
        if n1 == NZ:
            make(3, -3)
            next(main)
            make(2, -2)
        make(1, -1, 0)
        next(edge)
        next(main)
        loss_sum(losses, 2, NY)
        losses = loss_round(4, 6, x, xs)
        next(edge)
        if n1 == NZ:
            next(main)
        sent = next(main)
        next(second)
        for _ in range(n2 // 2 - 1):
            next(main)
            next(main)
            next(second)
        next(main)
        loss_sum(losses, 6, NX)
        losses = loss_round(7, 10, z, zs)
        sent += finish(edge)
        direct = [push(side.at[y, u], landing5.at[d], s7.at[d], r7.at[d], peer)
                  for d, (u, peer) in enumerate(zip(others, plane))]
        sent += finish(second)
        trade = [push(mine.at[pl.ds(lax.rem(y + d, NY) * sub, sub)], landing3.at[d - 1], s3.at[d - 1], r3.at[d - 1], peer)
                 for d, peer in enumerate(ys, 1)]
        for copy in trade:
            copy.wait_recv()
        ready[...] = mine[pl.ds(y * sub, sub)] + landing3[0] + landing3[1] + landing3[2]
        sent += share(ready, 0, MAIN, 0)
        for copy in direct:
            copy.wait_recv()
        found = side[y, users]
        for d in range(total - 1):
            found = found + landing5[d]
        last[...] = found
        sent += share(last, MAIN, found.shape[1], 4)
        loss_sum(losses, 10, NZ)
        for copy in sent + direct + trade:
            copy.wait_send()

    @pl.when(c == 0)
    def _():
        run(NZ, NX, z, x, lambda i1, i2: device(i2, y, i1, 0), lambda t: (t % NX) * NZ + t // NX)

    @pl.when(c == 1)
    def _():
        run(NX, NZ, x, z, lambda i1, i2: device(i1, y, i2, 1), lambda t: t)

    out[c, y, :, :MAIN] = ready[...]
    out[c, y, :, MAIN:] = last[...]
    loss_out[...] = sums[:1, :1]
    passed = []
    for base, start, width in ((0, 0, MAIN), (4, MAIN, last.shape[1])):
        for d in range(1, NY):
            ref = out.at[c, lax.rem(y + NY - d, NY), :, pl.ds(start, width)]
            pltpu.make_async_copy(ref, ref, r4.at[base + d]).wait()
            passed.append(push(ref, ref, s5.at[len(passed)], r5.at[len(passed)], partner))
    for base, start, width in ((0, 0, MAIN), (4, MAIN, last.shape[1])):
        ref = out.at[c, y, :, pl.ds(start, width)]
        pltpu.make_async_copy(ref, ref, r4.at[base]).wait()
    for copy in passed:
        copy.wait()


def reduce_rows(shares, narrow, slots, loss):
    pair, blocks, kb, half, width = shares.shape
    length, features = narrow.shape
    total = NX * NZ
    sub = half // NY
    edge = features - MAIN
    dma = pltpu.SemaphoreType.DMA
    f32 = jnp.float32
    anywhere = pl.BlockSpec(memory_space=pl.ANY)
    vmem = pl.BlockSpec(memory_space=pltpu.VMEM)
    out, loss = pl.pallas_call(
        reduce_kernel,
        in_specs=[anywhere, anywhere, pl.BlockSpec(memory_space=pltpu.SMEM), vmem],
        out_specs=[vmem, vmem],
        out_shape=(jax.ShapeDtypeStruct((2, NY, sub, features), f32), jax.ShapeDtypeStruct((1, 1), f32)),
        scratch_shapes=[
            pltpu.VMEM((pair * blocks, kb + 1, half, width), shares.dtype),
            pltpu.VMEM((pair * length, features), narrow.dtype),
            pltpu.VMEM((total, half, MAIN), f32),
            pltpu.VMEM((NY, total, sub, edge), f32),
            pltpu.VMEM((sub, MAIN), f32),
            pltpu.VMEM((sub, edge), f32),
            pltpu.VMEM((32, half, MAIN), f32),
            pltpu.VMEM((32, sub, MAIN), f32),
            pltpu.VMEM((4, sub, MAIN), f32),
            pltpu.VMEM((16, NZ, sub, edge), f32),
            pltpu.VMEM((total - 1, sub, edge), f32),
            pltpu.VMEM((2 + NY + NX + NZ,) + loss.shape, f32),
            pltpu.VMEM(loss.shape, f32),
            dma((2,)), dma((2,)), dma((2,)),
            dma((32,)), dma((32,)), dma((32,)), dma((32,)), dma((4,)), dma((4,)),
            dma((8,)), dma((8,)), dma((6,)), dma((6,)), dma((16,)), dma((16,)), dma((total - 1,)), dma((total - 1,)),
            dma((14,)), dma((14,)),
        ],
        compiler_params=pltpu.CompilerParams(collective_id=1, has_side_effects=True, vmem_limit_bytes=63 << 20),
        name="reduce",
    )(shares, narrow, slots, loss)
    return out.reshape(2 * half, features), loss.reshape(())


def per_device(hidden, target, pool_table, pool_items, labels, chosen, offsets):
    user_count = lax.axis_size("users")
    factor = 1.0 / (user_count * (offsets.shape[1] - 1))
    table, both = gather(pool_table, pool_items, chosen[0])
    grad_hidden, loss, shares, narrow, slots = score(
        hidden[0], target[0], labels[0], both, offsets[0], table, factor
    )
    grad_table, loss_total = reduce_rows(shares, narrow, slots, loss)
    return (loss_total, grad_hidden[None], grad_table)


def solution(mesh):
    return jax.shard_map(
        per_device,
        mesh=mesh,
        in_specs=(
            P("users", "seq", None),
            P("users", "seq", None),
            P("users", None),
            P("users"),
            P("users", "seq"),
            P("users", "seq", None),
            P("users", None),
        ),
        out_specs=(P(), P("users", "seq", None), P("users", None)),
        check_vma=False,
    )
```

```python
import functools
import jax
import jax.numpy as jnp
from jax import lax
from jax.experimental import pallas as pl
from jax.experimental.pallas import tpu as pltpu
from jax.sharding import PartitionSpec as P

MESH = pl.DeviceIdType.MESH
NX, NY, NZ = 4, 4, 8
EXTRA = 16


def where_am_i():
    seq, users = lax.axis_index("seq"), lax.axis_index("users")
    return users // NZ, seq // 2, users % NZ, seq % 2


def device(x, y, z, c):
    return {"seq": y * 2 + c, "users": x * NZ + z}


def greet(peers):
    barrier = pltpu.get_barrier_semaphore()
    for peer in peers:
        pl.semaphore_signal(barrier, inc=1, device_id=peer, device_id_type=MESH)
    pl.semaphore_wait(barrier, len(peers))


def push(src, dst, send_sem, recv_sem, to):
    copy = pltpu.make_async_remote_copy(src_ref=src, dst_ref=dst, send_sem=send_sem, recv_sem=recv_sem,
                                        device_id=to, device_id_type=MESH)
    copy.start()
    return copy


def gather_kernel(shard, items, chosen, table, both, whole, local_sem, pair_sem, partner_send, partner_recv, send1, recv1, send2, recv2):
    x, y, z, c = where_am_i()
    users = x * NZ + z
    total = NX * NZ
    rows = shard.shape[0]
    cut = rows // 2
    partner = device(x, y, z, 1 - c)

    whole[:rows] = shard[...]
    high = items[...] // 128
    digits = jnp.concatenate([high, items[...] - high * 128], axis=1).astype(jnp.float32)
    whole[rows:] = jnp.broadcast_to(digits, (EXTRA, digits.shape[1])).astype(whole.dtype)
    rows = rows + EXTRA

    greet([partner] + [device(lax.rem(x + d, NX), y, z, c) for d in range(1, NX)]
          + [device(x, y, lax.rem(z + d, NZ), c) for d in (1, NZ - 1)])
    mine = pltpu.make_async_copy(whole, table.at[users], local_sem.at[0])
    mine.start()
    mine_chosen = pltpu.make_async_copy(chosen, both.at[c], local_sem.at[1])
    mine_chosen.start()
    theirs = push(chosen, both.at[c], pair_sem.at[0], pair_sem.at[1], partner)

    def run(plan, n1, n2, me1, me2, start, count, where, dev):
        copies, pending = [], {}
        quarter = count // 2

        def region(i1, i2):
            return table.at[where(i1, i2), pl.ds(start, count)]

        def part(ref, h):
            return ref if h is None else ref.at[pl.ds(h * quarter, quarter)]

        def at(rel1, rel2):
            return region(lax.rem(me1 + rel1 + n1, n1), lax.rem(me2 + rel2 + n2, n2))

        def send(key, rel1, rel2, h, sems, to):
            dst = part(at(rel1, rel2), h)
            src = part(whole.at[pl.ds(start, count)], h) if rel1 == 0 and rel2 == 0 else dst
            pending[key] = push(src, dst, *sems, to)
            copies.append(pending[key])

        passed = []

        def arrive(key, rel1, rel2, h):
            pending.pop(key).wait_recv()
            ref = part(at(rel1, rel2), h)
            passed.append(push(ref, ref, partner_send.at[len(passed)], partner_recv, partner))

        ready = {0: 0}
        for stage, back, ahead, h in plan:
            ready[-back - ahead if abs(back + ahead) < n1 // 2 else n1 // 2] = stage
        stages = max(ready.values())
        for time in range(1, stages + n2 // 2 + 2):
            for i, (stage, back, ahead, h) in enumerate(plan):
                if stage == time - 1:
                    arrive((1, i), -back - ahead, 0, h)
            for i, (stage, back, ahead, h) in enumerate(plan):
                if stage == time:
                    send((1, i), -back, 0, h, (send1.at[i], recv1.at[i]), dev(lax.rem(me1 + ahead + n1, n1), me2))
            for sub, when in ready.items():
                s = time - when
                for d in (1, -1):
                    if 2 <= s <= n2 // 2 + 1:
                        h = None if s - 1 < n2 // 2 else int(d < 0)
                        arrive((2, sub, s - 1, d), sub, -d * (s - 1), h)
                    if 1 <= s <= n2 // 2:
                        h = None if s < n2 // 2 else int(d < 0)
                        k = ((sub % n1) * (n2 // 2) + s - 1) * 2 + (d < 0)
                        send((2, sub, s, d), sub, -d * (s - 1), h, (send2.at[k], recv2.at[k]),
                             dev(me1, lax.rem(me2 + d + n2, n2)))
        assert not pending
        for copy in copies + passed:
            copy.wait_send()
        rest = table.at[pl.ds(0, total - 1), pl.ds(0, start) if start else pl.ds(count, rows - count)]
        pltpu.make_async_copy(rest, rest, partner_recv).wait()

    across = [(1, 0, 1, None), (1, 0, -1, None), (1, 0, 2, None)]
    along = [(1, 0, 1, None), (1, 0, -1, None), (2, 1, 1, None), (2, -1, -1, None),
             (3, 2, 1, None), (3, -2, -1, None), (4, 3, 1, 0), (4, -3, -1, 1)]

    @pl.when(c == 0)
    def _():
        run(across, NX, NZ, x, z, 0, cut, lambda i1, i2: i1 * NZ + i2, lambda i1, i2: device(i1, y, i2, 0))

    @pl.when(c == 1)
    def _():
        run(along, NZ, NX, z, x, cut, rows - cut, lambda i1, i2: i2 * NZ + i1, lambda i1, i2: device(i2, y, i1, 1))

    mine.wait()
    mine_chosen.wait()
    theirs.wait()


def gather(pool_table, pool_items, chosen):
    rows, features = pool_table.shape
    total = NX * NZ
    dma = pltpu.SemaphoreType.DMA
    anywhere = pl.BlockSpec(memory_space=pl.ANY)
    table, both = pl.pallas_call(
        gather_kernel,
        in_specs=[pl.BlockSpec(memory_space=pltpu.VMEM)] * 3,
        out_specs=[anywhere] * 2,
        out_shape=(
            jax.ShapeDtypeStruct((total, rows + EXTRA, features), pool_table.dtype),
            jax.ShapeDtypeStruct((2,) + chosen.shape, chosen.dtype),
        ),
        scratch_shapes=[pltpu.VMEM((rows + EXTRA, features), pool_table.dtype),
                        dma((2,)), dma((2,)), dma((40,)), dma, dma((8,)), dma((8,)), dma((32,)),
                        dma((32,))],
        compiler_params=pltpu.CompilerParams(collective_id=0, has_side_effects=True),
        name="gather",
    )(pool_table, pool_items.reshape(1, rows), chosen)
    return table, both


NB = 256
PB = 128
TOGETHER = 2


def score_kernel(chosen_s, offsets_s, hidden_ref, target_ref, labels_ref, table_ref,
                 gh_ref, loss_ref, shares_ref, narrow_ref, slots_ref, scores, loss_acc, *, factor):
    step = pl.program_id(0)
    steps = pl.num_programs(0)
    pair, blocks, kb = chosen_s.shape
    count = table_ref.shape[0]
    hists = offsets_s.shape[0] - 1
    seq = lax.axis_index("seq")
    core = seq % 2

    for u in range(TOGETHER):
        b = step * TOGETHER + u
        for other in range(pair):
            for k in range(count):
                slots_ref[other * blocks + b, k] = kb
        for other in range(pair):
            for j in range(kb):
                slots_ref[other * blocks + b, chosen_s[other, b, j]] = j

    @pl.when(step == 0)
    def _():
        loss_acc[...] = jnp.zeros_like(loss_acc)

    first = (seq * blocks + step * TOGETHER) * PB
    live = first < offsets_s[hists]
    narrow_ref[...] = hidden_ref[...].astype(jnp.bfloat16)

    @pl.when(jnp.logical_not(live))
    def _():
        gh_ref[...] = jnp.zeros_like(gh_ref)
        shares_ref[...] = jnp.zeros_like(shares_ref)

    def look(u):
        b = step * TOGETHER + u
        rows = pl.ds(u * PB, PB)
        narrow = hidden_ref[rows].astype(jnp.bfloat16)
        positive = jnp.sum(narrow.astype(jnp.float32) * target_ref[rows].astype(jnp.float32), axis=1, keepdims=True)
        labels = jnp.broadcast_to(labels_ref[u].astype(jnp.float32), (PB, PB)).T[:, :1]
        top = jnp.full((PB, 128), -1e30, jnp.float32)
        for j in range(kb):
            k = chosen_s[core, b, j]
            digits = table_ref[k, NB:][:1].astype(jnp.float32)
            items = digits[:, :NB] * 128.0 + digits[:, NB:]
            raw = lax.dot_general(narrow, table_ref[k, :NB], (((1,), (1,)), ((), ())),
                                  preferred_element_type=jnp.float32)
            masked = jnp.where(items == labels, -1e30, raw)
            scores[u, :, j * NB:(j + 1) * NB] = masked
            for i in range(NB // 128):
                top = jnp.maximum(top, masked[:, i * 128:(i + 1) * 128])
        return positive, jnp.maximum(positive, jnp.max(top, axis=1, keepdims=True))

    def weigh(u, positive, peak):
        positions = first + u * PB + lax.broadcasted_iota(jnp.int32, (PB, 1), 0)
        weights = jnp.zeros((PB, 1), jnp.float32)
        for h in range(hists):
            start, finish = offsets_s[h], offsets_s[h + 1]
            length = jnp.broadcast_to(finish - start, (PB, 1)).astype(jnp.float32)
            inside = (positions >= start) & (positions < finish)
            weights = weights + jnp.where(inside, 1.0 / length, 0.0)
        added = jnp.zeros((PB, 128), jnp.float32)
        for j in range(kb):
            each = jnp.exp(scores[u, :, j * NB:(j + 1) * NB] - peak)
            scores[u, :, j * NB:(j + 1) * NB] = each
            for i in range(NB // 128):
                added = added + each[:, i * 128:(i + 1) * 128]
        pos_exp = jnp.exp(positive - peak)
        totals = pos_exp + jnp.sum(added, axis=1, keepdims=True)
        cross = peak + jnp.log(totals) - positive
        loss_acc[...] += jnp.broadcast_to(jnp.sum(weights * cross, axis=0, keepdims=True), loss_acc.shape)
        coeff = weights * factor
        return coeff / totals, coeff * (pos_exp / totals - 1.0)

    def pull(u, scale, pos_grad):
        b = step * TOGETHER + u
        rows = pl.ds(u * PB, PB)
        out = pos_grad * target_ref[rows].astype(jnp.float32)
        for j in range(kb):
            k = chosen_s[core, b, j]
            g = (scores[u, :, j * NB:(j + 1) * NB] * scale).astype(jnp.bfloat16)
            gt = g.T
            shares_ref[0, u, j] = gt[:PB]
            shares_ref[1, u, j] = gt[PB:]
            out = out + jnp.dot(g, table_ref[k, :NB], preferred_element_type=jnp.float32)
        gh_ref[rows] = out

    @pl.when(live)
    def _():
        seen = [look(0)]
        for u in range(TOGETHER):
            if u + 1 < TOGETHER:
                seen.append(look(u + 1))
            pull(u, *weigh(u, *seen[u]))

    @pl.when(step == steps - 1)
    def _():
        loss_ref[...] = loss_acc[...] * factor


def score(hidden, target, labels, chosen, offsets, table, factor):
    rows, features = hidden.shape
    blocks = rows // PB
    count = table.shape[0]
    pair, _, kb = chosen.shape
    half = NB // 2
    one = pl.Buffered(1)
    grid_spec = pltpu.PrefetchScalarGridSpec(
        num_scalar_prefetch=2,
        grid=(blocks // TOGETHER,),
        in_specs=[
            pl.BlockSpec((TOGETHER * PB, features), lambda b, *_: (b, 0)),
            pl.BlockSpec((TOGETHER * PB, features), lambda b, *_: (b, 0)),
            pl.BlockSpec((TOGETHER, 1, PB), lambda b, *_: (b, 0, 0)),
            pl.BlockSpec(table.shape, lambda b, *_: (0, 0, 0), pipeline_mode=one),
        ],
        out_specs=[
            pl.BlockSpec((TOGETHER * PB, features), lambda b, *_: (b, 0)),
            pl.BlockSpec((8, 128), lambda b, *_: (0, 0)),
            pl.BlockSpec((2, TOGETHER, kb, half, PB), lambda b, *_: (0, b, 0, 0, 0)),
            pl.BlockSpec((TOGETHER * PB, features), lambda b, *_: (b, 0)),
            pl.BlockSpec(memory_space=pltpu.SMEM),
        ],
        scratch_shapes=[
            pltpu.VMEM((TOGETHER, PB, kb * NB), jnp.float32),
            pltpu.VMEM((8, 128), jnp.float32),
        ],
    )
    return pl.pallas_call(
        functools.partial(score_kernel, factor=factor),
        grid_spec=grid_spec,
        out_shape=(
            jax.ShapeDtypeStruct((rows, features), jnp.float32),
            jax.ShapeDtypeStruct((8, 128), jnp.float32),
            jax.ShapeDtypeStruct((2, blocks, kb, half, PB), jnp.bfloat16),
            jax.ShapeDtypeStruct((rows, features), jnp.bfloat16),
            jax.ShapeDtypeStruct((pair * blocks, count), jnp.int32),
        ),
        compiler_params=pltpu.CompilerParams(vmem_limit_bytes=60 << 20),
        name="score",
    )(chosen, offsets, hidden, target, labels.reshape(blocks, 1, PB), table)


MAIN = 384


def reduce_kernel(shares, narrow, slots, loss_in, out, loss_out, lists, wide, own, side, ready, last, landing, landing2,
                  landing3, landing4, landing5, parts, sums, load_sem, pair_send, pair_recv, s1, r1, s2, r2, s3, r3,
                  s4, r4, s5, r5, s6, r6, s7, r7, loss_send, loss_recv):
    x, y, z, c = where_am_i()
    users = x * NZ + z
    total = NX * NZ
    partner = device(x, y, z, 1 - c)
    xs = [device(lax.rem(x + d, NX), y, z, c) for d in range(1, NX)]
    ys = [device(x, lax.rem(y + d, NY), z, c) for d in range(1, NY)]
    zs = [device(x, y, lax.rem(z + d, NZ), c) for d in range(1, NZ)]
    others = [lax.rem(users + d, total) for d in range(1, total)]
    plane = [{"seq": y * 2 + c, "users": u} for u in others]
    blocks, kb = shares.shape[1:3]
    rows = own.shape[1]
    sub = rows // NY
    length = narrow.shape[0]

    def loss_round(k, base, me, peers):
        parts[base + me] = sums[...]
        return [push(sums, parts.at[base + me], loss_send.at[k + d], loss_recv.at[k + d], peer)
                for d, peer in enumerate(peers)]

    def loss_sum(copies, base, count):
        for copy in copies:
            copy.wait()
        added = parts[base]
        for i in range(1, count):
            added = added + parts[base + i]
        sums[...] = added

    sums[...] = loss_in[...]
    greet([partner] + ys + plane)
    losses = loss_round(0, 0, c, [partner])
    pair = [
        push(shares.at[1 - c], lists.at[pl.ds(c * blocks, blocks), pl.ds(0, kb)], pair_send.at[0], pair_recv.at[0], partner),
        push(narrow, wide.at[pl.ds(c * length, length)], pair_send.at[1], pair_recv.at[1], partner),
        pltpu.make_async_copy(shares.at[c], lists.at[pl.ds(c * blocks, blocks), pl.ds(0, kb)], load_sem.at[0]),
        pltpu.make_async_copy(narrow, wide.at[pl.ds(c * length, length)], load_sem.at[1]),
    ]
    for copy in pair[2:]:
        copy.start()
    for i in range(2 * blocks):
        lists[i, kb] = jnp.zeros(lists.shape[2:], lists.dtype)
    loss_sum(losses, 0, 2)
    for copy in pair:
        copy.wait()

    def half(ref, h):
        size = ref.shape[0] // 2
        return ref.at[pl.ds(h * size, size)]

    def add(dst, src):
        step = min(dst.shape[0], 64 if len(dst.shape) == 2 else 4)

        @pl.loop(0, dst.shape[0] // step)
        def _(i):
            here = pl.ds(pl.multiple_of(i * step, step), step)
            dst[here] += src[here]

    def tree(n, me, order, chunk, land, send_sems, recv_sems, up, down, fine=False):
        old = {}
        subs = len(order)
        for s in range(1, n // 2 + 2):
            ahead = n // 2 + 1 - s
            for i, j in enumerate(order):
                for d, to in ((1, up), (-1, down)):
                    ref = chunk(lax.rem(me + d * ahead + n, n), j)
                    if s > 1:
                        slot = ((s - 2) * subs + i) * 2 + (d < 0)
                        old[slot].wait_recv()
                        if s == 2:
                            add(half(ref, d < 0), half(land.at[slot], d < 0))
                        else:
                            add(ref, land.at[slot])
                    if ahead:
                        slot = ((s - 1) * subs + i) * 2 + (d < 0)
                        dst = land.at[slot]
                        if s == 1:
                            ref, dst = half(ref, d < 0), half(dst, d < 0)
                        old[slot] = push(ref, dst, send_sems.at[slot], recv_sems.at[slot], to)
                if fine and not ahead:
                    yield list(old.values())
            if ahead or not fine:
                yield list(old.values())

    def finish(steps):
        for copies in steps:
            pass
        return copies

    def share(ref, start, width, base):
        done = out.at[c, y, :, pl.ds(start, width)]
        return [push(ref, done, s4.at[base + d], r4.at[base + d], peer) for d, peer in enumerate([partner] + ys)]

    group = 4

    def produce(first, count, block):
        @pl.loop(0, count)
        def _(g):
            base = (first + g) * group
            lhs = []
            for i in range(group):
                k = block(base + i)
                lhs.append(jnp.concatenate([lists[b, slots[b, k]] for b in range(2 * blocks)], axis=1))
            found = jnp.dot(jnp.concatenate(lhs, axis=0), wide[...], preferred_element_type=jnp.float32)
            for i in range(group):
                own[base + i] = found[i * rows:(i + 1) * rows, :MAIN]
                for w in range(NY):
                    side[w, block(base + i)] = found[i * rows + w * sub:i * rows + (w + 1) * sub, MAIN:]

    def run(n1, n2, me1, me2, dev, block):
        per = n2 // group

        def make(*places):
            for place in places:
                produce(lax.rem(me1 + place + n1, n1) * per, per, block)

        reach = [n2 // 2] + [r for q in range(n2 // 2 - 1, 0, -1) for r in (q, -q)] + [0]
        main = tree(n1, me1, [lax.rem(me2 + r + n2, n2) for r in reach], lambda i1, j: own.at[i1 * n2 + j], landing,
                    s1, r1, dev(lax.rem(me1 + 1, n1), me2), dev(lax.rem(me1 + n1 - 1, n1), me2), fine=True)
        edge = tree(NY, y, range(NX), lambda i, j: side.at[i, pl.ds(j * NZ, NZ)], landing4, s6, r6, ys[0], ys[-1])
        second = tree(n2, me2, range(NY), lambda i, j: own.at[me1 * n2 + i, pl.ds(j * sub, sub)], landing2, s2, r2,
                      dev(me1, lax.rem(me2 + 1, n2)), dev(me1, lax.rem(me2 + n2 - 1, n2)))
        mine = own.at[me1 * n2 + me2]
        make(n1 // 2)
        next(main)
        losses = loss_round(1, 2, y, ys)
        if n1 == NZ:
            make(3, -3)
            next(main)
            make(2, -2)
        make(1, -1, 0)
        next(edge)
        next(main)
        loss_sum(losses, 2, NY)
        losses = loss_round(4, 6, x, xs)
        next(edge)
        if n1 == NZ:
            next(main)
        sent = next(main)
        next(second)
        for _ in range(n2 // 2 - 1):
            next(main)
            next(main)
            next(second)
        next(main)
        loss_sum(losses, 6, NX)
        losses = loss_round(7, 10, z, zs)
        sent += finish(edge)
        direct = [push(side.at[y, u], landing5.at[d], s7.at[d], r7.at[d], peer)
                  for d, (u, peer) in enumerate(zip(others, plane))]
        sent += finish(second)
        trade = [push(mine.at[pl.ds(lax.rem(y + d, NY) * sub, sub)], landing3.at[d - 1], s3.at[d - 1], r3.at[d - 1], peer)
                 for d, peer in enumerate(ys, 1)]
        for copy in trade:
            copy.wait_recv()
        ready[...] = mine[pl.ds(y * sub, sub)] + landing3[0] + landing3[1] + landing3[2]
        sent += share(ready, 0, MAIN, 0)
        for copy in direct:
            copy.wait_recv()
        found = side[y, users]
        for d in range(total - 1):
            found = found + landing5[d]
        last[...] = found
        sent += share(last, MAIN, found.shape[1], 4)
        loss_sum(losses, 10, NZ)
        for copy in sent + direct + trade:
            copy.wait_send()

    @pl.when(c == 0)
    def _():
        run(NZ, NX, z, x, lambda i1, i2: device(i2, y, i1, 0), lambda t: (t % NX) * NZ + t // NX)

    @pl.when(c == 1)
    def _():
        run(NX, NZ, x, z, lambda i1, i2: device(i1, y, i2, 1), lambda t: t)

    out[c, y, :, :MAIN] = ready[...]
    out[c, y, :, MAIN:] = last[...]
    loss_out[...] = sums[:1, :1]
    passed = []
    for base, start, width in ((0, 0, MAIN), (4, MAIN, last.shape[1])):
        for d in range(1, NY):
            ref = out.at[c, lax.rem(y + NY - d, NY), :, pl.ds(start, width)]
            pltpu.make_async_copy(ref, ref, r4.at[base + d]).wait()
            passed.append(push(ref, ref, s5.at[len(passed)], r5.at[len(passed)], partner))
    for base, start, width in ((0, 0, MAIN), (4, MAIN, last.shape[1])):
        ref = out.at[c, y, :, pl.ds(start, width)]
        pltpu.make_async_copy(ref, ref, r4.at[base]).wait()
    for copy in passed:
        copy.wait()


def reduce_rows(shares, narrow, slots, loss):
    pair, blocks, kb, half, width = shares.shape
    length, features = narrow.shape
    total = NX * NZ
    sub = half // NY
    edge = features - MAIN
    dma = pltpu.SemaphoreType.DMA
    f32 = jnp.float32
    anywhere = pl.BlockSpec(memory_space=pl.ANY)
    vmem = pl.BlockSpec(memory_space=pltpu.VMEM)
    out, loss = pl.pallas_call(
        reduce_kernel,
        in_specs=[anywhere, anywhere, pl.BlockSpec(memory_space=pltpu.SMEM), vmem],
        out_specs=[vmem, vmem],
        out_shape=(jax.ShapeDtypeStruct((2, NY, sub, features), f32), jax.ShapeDtypeStruct((1, 1), f32)),
        scratch_shapes=[
            pltpu.VMEM((pair * blocks, kb + 1, half, width), shares.dtype),
            pltpu.VMEM((pair * length, features), narrow.dtype),
            pltpu.VMEM((total, half, MAIN), f32),
            pltpu.VMEM((NY, total, sub, edge), f32),
            pltpu.VMEM((sub, MAIN), f32),
            pltpu.VMEM((sub, edge), f32),
            pltpu.VMEM((32, half, MAIN), f32),
            pltpu.VMEM((32, sub, MAIN), f32),
            pltpu.VMEM((4, sub, MAIN), f32),
            pltpu.VMEM((16, NZ, sub, edge), f32),
            pltpu.VMEM((total - 1, sub, edge), f32),
            pltpu.VMEM((2 + NY + NX + NZ,) + loss.shape, f32),
            pltpu.VMEM(loss.shape, f32),
            dma((2,)), dma((2,)), dma((2,)),
            dma((32,)), dma((32,)), dma((32,)), dma((32,)), dma((4,)), dma((4,)),
            dma((8,)), dma((8,)), dma((6,)), dma((6,)), dma((16,)), dma((16,)), dma((total - 1,)), dma((total - 1,)),
            dma((14,)), dma((14,)),
        ],
        compiler_params=pltpu.CompilerParams(collective_id=1, has_side_effects=True, vmem_limit_bytes=63 << 20),
        name="reduce",
    )(shares, narrow, slots, loss)
    return out.reshape(2 * half, features), loss.reshape(())


def per_device(hidden, target, pool_table, pool_items, labels, chosen, offsets):
    user_count = lax.axis_size("users")
    factor = 1.0 / (user_count * (offsets.shape[1] - 1))
    table, both = gather(pool_table, pool_items, chosen[0])
    grad_hidden, loss, shares, narrow, slots = score(
        hidden[0], target[0], labels[0], both, offsets[0], table, factor
    )
    grad_table, loss_total = reduce_rows(shares, narrow, slots, loss)
    return (loss_total, grad_hidden[None], grad_table)


def solution(mesh):
    return jax.shard_map(
        per_device,
        mesh=mesh,
        in_specs=(
            P("users", "seq", None),
            P("users", "seq", None),
            P("users", None),
            P("users"),
            P("users", "seq"),
            P("users", "seq", None),
            P("users", None),
        ),
        out_specs=(P(), P("users", "seq", None), P("users", None)),
        check_vma=False,
    )
```

```python
import functools
import jax
import jax.numpy as jnp
from jax import lax
from jax.experimental import pallas as pl
from jax.experimental.pallas import tpu as pltpu
from jax.sharding import PartitionSpec as P

MESH = pl.DeviceIdType.MESH
NX, NY, NZ = 4, 4, 8
EXTRA = 16


def where_am_i():
    seq, users = lax.axis_index("seq"), lax.axis_index("users")
    return users // NZ, seq // 2, users % NZ, seq % 2


def device(x, y, z, c):
    return {"seq": y * 2 + c, "users": x * NZ + z}


def greet(peers):
    barrier = pltpu.get_barrier_semaphore()
    for peer in peers:
        pl.semaphore_signal(barrier, inc=1, device_id=peer, device_id_type=MESH)
    pl.semaphore_wait(barrier, len(peers))


def push(src, dst, send_sem, recv_sem, to):
    copy = pltpu.make_async_remote_copy(src_ref=src, dst_ref=dst, send_sem=send_sem, recv_sem=recv_sem,
                                        device_id=to, device_id_type=MESH)
    copy.start()
    return copy


def gather_kernel(shard, items, chosen, table, both, whole, local_sem, pair_sem, partner_send, partner_recv, send1, recv1, send2, recv2):
    x, y, z, c = where_am_i()
    users = x * NZ + z
    total = NX * NZ
    rows = shard.shape[0]
    cut = rows // 2
    partner = device(x, y, z, 1 - c)

    whole[:rows] = shard[...]
    high = items[...] // 128
    digits = jnp.concatenate([high, items[...] - high * 128], axis=1).astype(jnp.float32)
    whole[rows:] = jnp.broadcast_to(digits, (EXTRA, digits.shape[1])).astype(whole.dtype)
    rows = rows + EXTRA

    greet([partner] + [device(lax.rem(x + d, NX), y, z, c) for d in range(1, NX)]
          + [device(x, y, lax.rem(z + d, NZ), c) for d in (1, NZ - 1)])
    mine = pltpu.make_async_copy(whole, table.at[users], local_sem.at[0])
    mine.start()
    mine_chosen = pltpu.make_async_copy(chosen, both.at[c], local_sem.at[1])
    mine_chosen.start()
    theirs = push(chosen, both.at[c], pair_sem.at[0], pair_sem.at[1], partner)

    def run(plan, n1, n2, me1, me2, start, count, where, dev):
        copies, pending = [], {}
        quarter = count // 2

        def region(i1, i2):
            return table.at[where(i1, i2), pl.ds(start, count)]

        def part(ref, h):
            return ref if h is None else ref.at[pl.ds(h * quarter, quarter)]

        def at(rel1, rel2):
            return region(lax.rem(me1 + rel1 + n1, n1), lax.rem(me2 + rel2 + n2, n2))

        def send(key, rel1, rel2, h, sems, to):
            dst = part(at(rel1, rel2), h)
            src = part(whole.at[pl.ds(start, count)], h) if rel1 == 0 and rel2 == 0 else dst
            pending[key] = push(src, dst, *sems, to)
            copies.append(pending[key])

        passed = []

        def arrive(key, rel1, rel2, h):
            pending.pop(key).wait_recv()
            ref = part(at(rel1, rel2), h)
            passed.append(push(ref, ref, partner_send.at[len(passed)], partner_recv, partner))

        ready = {0: 0}
        for stage, back, ahead, h in plan:
            ready[-back - ahead if abs(back + ahead) < n1 // 2 else n1 // 2] = stage
        stages = max(ready.values())
        for time in range(1, stages + n2 // 2 + 2):
            for i, (stage, back, ahead, h) in enumerate(plan):
                if stage == time - 1:
                    arrive((1, i), -back - ahead, 0, h)
            for i, (stage, back, ahead, h) in enumerate(plan):
                if stage == time:
                    send((1, i), -back, 0, h, (send1.at[i], recv1.at[i]), dev(lax.rem(me1 + ahead + n1, n1), me2))
            for sub, when in ready.items():
                s = time - when
                for d in (1, -1):
                    if 2 <= s <= n2 // 2 + 1:
                        h = None if s - 1 < n2 // 2 else int(d < 0)
                        arrive((2, sub, s - 1, d), sub, -d * (s - 1), h)
                    if 1 <= s <= n2 // 2:
                        h = None if s < n2 // 2 else int(d < 0)
                        k = ((sub % n1) * (n2 // 2) + s - 1) * 2 + (d < 0)
                        send((2, sub, s, d), sub, -d * (s - 1), h, (send2.at[k], recv2.at[k]),
                             dev(me1, lax.rem(me2 + d + n2, n2)))
        assert not pending
        for copy in copies + passed:
            copy.wait_send()
        rest = table.at[pl.ds(0, total - 1), pl.ds(0, start) if start else pl.ds(count, rows - count)]
        pltpu.make_async_copy(rest, rest, partner_recv).wait()

    across = [(1, 0, 1, None), (1, 0, -1, None), (1, 0, 2, None)]
    along = [(1, 0, 1, None), (1, 0, -1, None), (2, 1, 1, None), (2, -1, -1, None),
             (3, 2, 1, None), (3, -2, -1, None), (4, 3, 1, 0), (4, -3, -1, 1)]

    @pl.when(c == 0)
    def _():
        run(across, NX, NZ, x, z, 0, cut, lambda i1, i2: i1 * NZ + i2, lambda i1, i2: device(i1, y, i2, 0))

    @pl.when(c == 1)
    def _():
        run(along, NZ, NX, z, x, cut, rows - cut, lambda i1, i2: i2 * NZ + i1, lambda i1, i2: device(i2, y, i1, 1))

    mine.wait()
    mine_chosen.wait()
    theirs.wait()


def gather(pool_table, pool_items, chosen):
    rows, features = pool_table.shape
    total = NX * NZ
    dma = pltpu.SemaphoreType.DMA
    anywhere = pl.BlockSpec(memory_space=pl.ANY)
    table, both = pl.pallas_call(
        gather_kernel,
        in_specs=[pl.BlockSpec(memory_space=pltpu.VMEM)] * 3,
        out_specs=[anywhere] * 2,
        out_shape=(
            jax.ShapeDtypeStruct((total, rows + EXTRA, features), pool_table.dtype),
            jax.ShapeDtypeStruct((2,) + chosen.shape, chosen.dtype),
        ),
        scratch_shapes=[pltpu.VMEM((rows + EXTRA, features), pool_table.dtype),
                        dma((2,)), dma((2,)), dma((40,)), dma, dma((8,)), dma((8,)), dma((32,)),
                        dma((32,))],
        compiler_params=pltpu.CompilerParams(collective_id=0, has_side_effects=True),
        name="gather",
    )(pool_table, pool_items.reshape(1, rows), chosen)
    return table, both


NB = 256
PB = 128
TOGETHER = 2


def score_kernel(chosen_s, offsets_s, hidden_ref, target_ref, labels_ref, table_ref,
                 gh_ref, loss_ref, shares_ref, narrow_ref, slots_ref, scores, loss_acc, *, factor):
    step = pl.program_id(0)
    steps = pl.num_programs(0)
    pair, blocks, kb = chosen_s.shape
    count = table_ref.shape[0]
    hists = offsets_s.shape[0] - 1
    seq = lax.axis_index("seq")
    core = seq % 2

    for u in range(TOGETHER):
        b = step * TOGETHER + u
        for other in range(pair):
            for k in range(count):
                slots_ref[other * blocks + b, k] = kb
        for other in range(pair):
            for j in range(kb):
                slots_ref[other * blocks + b, chosen_s[other, b, j]] = j

    @pl.when(step == 0)
    def _():
        loss_acc[...] = jnp.zeros_like(loss_acc)

    first = (seq * blocks + step * TOGETHER) * PB
    live = first < offsets_s[hists]
    narrow_ref[...] = hidden_ref[...].astype(jnp.bfloat16)

    @pl.when(jnp.logical_not(live))
    def _():
        gh_ref[...] = jnp.zeros_like(gh_ref)
        shares_ref[...] = jnp.zeros_like(shares_ref)

    def look(u):
        b = step * TOGETHER + u
        rows = pl.ds(u * PB, PB)
        narrow = hidden_ref[rows].astype(jnp.bfloat16)
        positive = jnp.sum(narrow.astype(jnp.float32) * target_ref[rows].astype(jnp.float32), axis=1, keepdims=True)
        labels = jnp.broadcast_to(labels_ref[u].astype(jnp.float32), (PB, PB)).T[:, :1]
        top = jnp.full((PB, 128), -1e30, jnp.float32)
        for j in range(kb):
            k = chosen_s[core, b, j]
            digits = table_ref[k, NB:][:1].astype(jnp.float32)
            items = digits[:, :NB] * 128.0 + digits[:, NB:]
            raw = lax.dot_general(narrow, table_ref[k, :NB], (((1,), (1,)), ((), ())),
                                  preferred_element_type=jnp.float32)
            masked = jnp.where(items == labels, -1e30, raw)
            scores[u, :, j * NB:(j + 1) * NB] = masked
            for i in range(NB // 128):
                top = jnp.maximum(top, masked[:, i * 128:(i + 1) * 128])
        return positive, jnp.maximum(positive, jnp.max(top, axis=1, keepdims=True))

    def weigh(u, positive, peak):
        positions = first + u * PB + lax.broadcasted_iota(jnp.int32, (PB, 1), 0)
        weights = jnp.zeros((PB, 1), jnp.float32)
        for h in range(hists):
            start, finish = offsets_s[h], offsets_s[h + 1]
            length = jnp.broadcast_to(finish - start, (PB, 1)).astype(jnp.float32)
            inside = (positions >= start) & (positions < finish)
            weights = weights + jnp.where(inside, 1.0 / length, 0.0)
        added = jnp.zeros((PB, 128), jnp.float32)
        for j in range(kb):
            each = jnp.exp(scores[u, :, j * NB:(j + 1) * NB] - peak)
            scores[u, :, j * NB:(j + 1) * NB] = each
            for i in range(NB // 128):
                added = added + each[:, i * 128:(i + 1) * 128]
        pos_exp = jnp.exp(positive - peak)
        totals = pos_exp + jnp.sum(added, axis=1, keepdims=True)
        cross = peak + jnp.log(totals) - positive
        loss_acc[...] += jnp.broadcast_to(jnp.sum(weights * cross, axis=0, keepdims=True), loss_acc.shape)
        coeff = weights * factor
        return coeff / totals, coeff * (pos_exp / totals - 1.0)

    def pull(u, scale, pos_grad):
        b = step * TOGETHER + u
        rows = pl.ds(u * PB, PB)
        out = pos_grad * target_ref[rows].astype(jnp.float32)
        for j in range(kb):
            k = chosen_s[core, b, j]
            g = (scores[u, :, j * NB:(j + 1) * NB] * scale).astype(jnp.bfloat16)
            gt = g.T
            shares_ref[0, u, j] = gt[:PB]
            shares_ref[1, u, j] = gt[PB:]
            out = out + jnp.dot(g, table_ref[k, :NB], preferred_element_type=jnp.float32)
        gh_ref[rows] = out

    @pl.when(live)
    def _():
        seen = [look(0)]
        for u in range(TOGETHER):
            if u + 1 < TOGETHER:
                seen.append(look(u + 1))
            pull(u, *weigh(u, *seen[u]))

    @pl.when(step == steps - 1)
    def _():
        loss_ref[...] = loss_acc[...] * factor


def score(hidden, target, labels, chosen, offsets, table, factor):
    rows, features = hidden.shape
    blocks = rows // PB
    count = table.shape[0]
    pair, _, kb = chosen.shape
    half = NB // 2
    one = pl.Buffered(1)
    grid_spec = pltpu.PrefetchScalarGridSpec(
        num_scalar_prefetch=2,
        grid=(blocks // TOGETHER,),
        in_specs=[
            pl.BlockSpec((TOGETHER * PB, features), lambda b, *_: (b, 0)),
            pl.BlockSpec((TOGETHER * PB, features), lambda b, *_: (b, 0)),
            pl.BlockSpec((TOGETHER, 1, PB), lambda b, *_: (b, 0, 0)),
            pl.BlockSpec(table.shape, lambda b, *_: (0, 0, 0), pipeline_mode=one),
        ],
        out_specs=[
            pl.BlockSpec((TOGETHER * PB, features), lambda b, *_: (b, 0)),
            pl.BlockSpec((8, 128), lambda b, *_: (0, 0)),
            pl.BlockSpec((2, TOGETHER, kb, half, PB), lambda b, *_: (0, b, 0, 0, 0)),
            pl.BlockSpec((TOGETHER * PB, features), lambda b, *_: (b, 0)),
            pl.BlockSpec(memory_space=pltpu.SMEM),
        ],
        scratch_shapes=[
            pltpu.VMEM((TOGETHER, PB, kb * NB), jnp.float32),
            pltpu.VMEM((8, 128), jnp.float32),
        ],
    )
    return pl.pallas_call(
        functools.partial(score_kernel, factor=factor),
        grid_spec=grid_spec,
        out_shape=(
            jax.ShapeDtypeStruct((rows, features), jnp.float32),
            jax.ShapeDtypeStruct((8, 128), jnp.float32),
            jax.ShapeDtypeStruct((2, blocks, kb, half, PB), jnp.bfloat16),
            jax.ShapeDtypeStruct((rows, features), jnp.bfloat16),
            jax.ShapeDtypeStruct((pair * blocks, count), jnp.int32),
        ),
        compiler_params=pltpu.CompilerParams(vmem_limit_bytes=60 << 20),
        name="score",
    )(chosen, offsets, hidden, target, labels.reshape(blocks, 1, PB), table)


MAIN = 384


def reduce_kernel(shares, narrow, slots, loss_in, out, loss_out, lists, wide, own, side, ready, last, landing, landing2,
                  landing3, landing4, landing5, parts, sums, load_sem, pair_send, pair_recv, s1, r1, s2, r2, s3, r3,
                  s4, r4, s5, r5, s6, r6, s7, r7, loss_send, loss_recv):
    x, y, z, c = where_am_i()
    users = x * NZ + z
    total = NX * NZ
    partner = device(x, y, z, 1 - c)
    xs = [device(lax.rem(x + d, NX), y, z, c) for d in range(1, NX)]
    ys = [device(x, lax.rem(y + d, NY), z, c) for d in range(1, NY)]
    zs = [device(x, y, lax.rem(z + d, NZ), c) for d in range(1, NZ)]
    others = [lax.rem(users + d, total) for d in range(1, total)]
    plane = [{"seq": y * 2 + c, "users": u} for u in others]
    blocks, kb = shares.shape[1:3]
    rows = own.shape[1]
    sub = rows // NY
    length = narrow.shape[0]

    def loss_round(k, base, me, peers):
        parts[base + me] = sums[...]
        return [push(sums, parts.at[base + me], loss_send.at[k + d], loss_recv.at[k + d], peer)
                for d, peer in enumerate(peers)]

    def loss_sum(copies, base, count):
        for copy in copies:
            copy.wait()
        added = parts[base]
        for i in range(1, count):
            added = added + parts[base + i]
        sums[...] = added

    sums[...] = loss_in[...]
    loads = [
        pltpu.make_async_copy(shares.at[c], lists.at[pl.ds(c * blocks, blocks), pl.ds(0, kb)], load_sem.at[0]),
        pltpu.make_async_copy(narrow, wide.at[pl.ds(c * length, length)], load_sem.at[1]),
    ]
    for copy in loads:
        copy.start()
    for i in range(2 * blocks):
        lists[i, kb] = jnp.zeros(lists.shape[2:], lists.dtype)
    greet([partner] + ys + plane)
    losses = loss_round(0, 0, c, [partner])
    pair = [
        push(shares.at[1 - c], lists.at[pl.ds(c * blocks, blocks), pl.ds(0, kb)], pair_send.at[0], pair_recv.at[0], partner),
        push(narrow, wide.at[pl.ds(c * length, length)], pair_send.at[1], pair_recv.at[1], partner),
    ] + loads
    loss_sum(losses, 0, 2)
    for copy in pair:
        copy.wait()

    def half(ref, h):
        size = ref.shape[0] // 2
        return ref.at[pl.ds(h * size, size)]

    def add(dst, src):
        step = min(dst.shape[0], 64 if len(dst.shape) == 2 else 4)

        @pl.loop(0, dst.shape[0] // step)
        def _(i):
            here = pl.ds(pl.multiple_of(i * step, step), step)
            dst[here] += src[here]

    def tree(n, me, order, chunk, land, send_sems, recv_sems, up, down, fine=False):
        old = {}
        subs = len(order)
        for s in range(1, n // 2 + 2):
            ahead = n // 2 + 1 - s
            for i, j in enumerate(order):
                for d, to in ((1, up), (-1, down)):
                    ref = chunk(lax.rem(me + d * ahead + n, n), j)
                    if s > 1:
                        slot = ((s - 2) * subs + i) * 2 + (d < 0)
                        old[slot].wait_recv()
                        if s == 2:
                            add(half(ref, d < 0), half(land.at[slot], d < 0))
                        else:
                            add(ref, land.at[slot])
                    if ahead:
                        slot = ((s - 1) * subs + i) * 2 + (d < 0)
                        dst = land.at[slot]
                        if s == 1:
                            ref, dst = half(ref, d < 0), half(dst, d < 0)
                        old[slot] = push(ref, dst, send_sems.at[slot], recv_sems.at[slot], to)
                if fine and not ahead:
                    yield list(old.values())
            if ahead or not fine:
                yield list(old.values())

    def finish(steps):
        for copies in steps:
            pass
        return copies

    def share(ref, start, width, base):
        done = out.at[c, y, :, pl.ds(start, width)]
        return [push(ref, done, s4.at[base + d], r4.at[base + d], peer) for d, peer in enumerate([partner] + ys)]

    group = 4

    def produce(first, count, block):
        @pl.loop(0, count)
        def _(g):
            base = (first + g) * group
            lhs = []
            for i in range(group):
                k = block(base + i)
                lhs.append(jnp.concatenate([lists[b, slots[b, k]] for b in range(2 * blocks)], axis=1))
            found = jnp.dot(jnp.concatenate(lhs, axis=0), wide[...], preferred_element_type=jnp.float32)
            for i in range(group):
                own[base + i] = found[i * rows:(i + 1) * rows, :MAIN]
                for w in range(NY):
                    side[w, block(base + i)] = found[i * rows + w * sub:i * rows + (w + 1) * sub, MAIN:]

    def run(n1, n2, me1, me2, dev, block):
        per = n2 // group

        def make(*places):
            for place in places:
                produce(lax.rem(me1 + place + n1, n1) * per, per, block)

        reach = [n2 // 2] + [r for q in range(n2 // 2 - 1, 0, -1) for r in (q, -q)] + [0]
        main = tree(n1, me1, [lax.rem(me2 + r + n2, n2) for r in reach], lambda i1, j: own.at[i1 * n2 + j], landing,
                    s1, r1, dev(lax.rem(me1 + 1, n1), me2), dev(lax.rem(me1 + n1 - 1, n1), me2), fine=True)
        edge = tree(NY, y, range(NX), lambda i, j: side.at[i, pl.ds(j * NZ, NZ)], landing4, s6, r6, ys[0], ys[-1])
        second = tree(n2, me2, range(NY), lambda i, j: own.at[me1 * n2 + i, pl.ds(j * sub, sub)], landing2, s2, r2,
                      dev(me1, lax.rem(me2 + 1, n2)), dev(me1, lax.rem(me2 + n2 - 1, n2)))
        mine = own.at[me1 * n2 + me2]
        make(n1 // 2)
        next(main)
        losses = loss_round(1, 2, y, ys)
        if n1 == NZ:
            make(3, -3)
            next(main)
            make(2, -2)
        make(1, -1, 0)
        next(edge)
        next(main)
        loss_sum(losses, 2, NY)
        losses = loss_round(4, 6, x, xs)
        next(edge)
        if n1 == NZ:
            next(main)
        sent = next(main)
        next(second)
        for _ in range(n2 // 2 - 1):
            next(main)
            next(main)
            next(second)
        next(main)
        loss_sum(losses, 6, NX)
        losses = loss_round(7, 10, z, zs)
        sent += finish(edge)
        direct = [push(side.at[y, u], landing5.at[d], s7.at[d], r7.at[d], peer)
                  for d, (u, peer) in enumerate(zip(others, plane))]
        sent += finish(second)
        trade = [push(mine.at[pl.ds(lax.rem(y + d, NY) * sub, sub)], landing3.at[d - 1], s3.at[d - 1], r3.at[d - 1], peer)
                 for d, peer in enumerate(ys, 1)]
        for copy in trade:
            copy.wait_recv()
        ready[...] = mine[pl.ds(y * sub, sub)] + landing3[0] + landing3[1] + landing3[2]
        sent += share(ready, 0, MAIN, 0)
        for copy in direct:
            copy.wait_recv()
        found = side[y, users]
        for d in range(total - 1):
            found = found + landing5[d]
        last[...] = found
        sent += share(last, MAIN, found.shape[1], 4)
        loss_sum(losses, 10, NZ)
        for copy in sent + direct + trade:
            copy.wait_send()

    @pl.when(c == 0)
    def _():
        run(NZ, NX, z, x, lambda i1, i2: device(i2, y, i1, 0), lambda t: (t % NX) * NZ + t // NX)

    @pl.when(c == 1)
    def _():
        run(NX, NZ, x, z, lambda i1, i2: device(i1, y, i2, 1), lambda t: t)

    out[c, y, :, :MAIN] = ready[...]
    out[c, y, :, MAIN:] = last[...]
    loss_out[...] = sums[:1, :1]
    passed = []
    for base, start, width in ((0, 0, MAIN), (4, MAIN, last.shape[1])):
        for d in range(1, NY):
            ref = out.at[c, lax.rem(y + NY - d, NY), :, pl.ds(start, width)]
            pltpu.make_async_copy(ref, ref, r4.at[base + d]).wait()
            passed.append(push(ref, ref, s5.at[len(passed)], r5.at[len(passed)], partner))
    for base, start, width in ((0, 0, MAIN), (4, MAIN, last.shape[1])):
        ref = out.at[c, y, :, pl.ds(start, width)]
        pltpu.make_async_copy(ref, ref, r4.at[base]).wait()
    for copy in passed:
        copy.wait()


def reduce_rows(shares, narrow, slots, loss):
    pair, blocks, kb, half, width = shares.shape
    length, features = narrow.shape
    total = NX * NZ
    sub = half // NY
    edge = features - MAIN
    dma = pltpu.SemaphoreType.DMA
    f32 = jnp.float32
    anywhere = pl.BlockSpec(memory_space=pl.ANY)
    vmem = pl.BlockSpec(memory_space=pltpu.VMEM)
    out, loss = pl.pallas_call(
        reduce_kernel,
        in_specs=[anywhere, anywhere, pl.BlockSpec(memory_space=pltpu.SMEM), vmem],
        out_specs=[vmem, vmem],
        out_shape=(jax.ShapeDtypeStruct((2, NY, sub, features), f32), jax.ShapeDtypeStruct((1, 1), f32)),
        scratch_shapes=[
            pltpu.VMEM((pair * blocks, kb + 1, half, width), shares.dtype),
            pltpu.VMEM((pair * length, features), narrow.dtype),
            pltpu.VMEM((total, half, MAIN), f32),
            pltpu.VMEM((NY, total, sub, edge), f32),
            pltpu.VMEM((sub, MAIN), f32),
            pltpu.VMEM((sub, edge), f32),
            pltpu.VMEM((32, half, MAIN), f32),
            pltpu.VMEM((32, sub, MAIN), f32),
            pltpu.VMEM((4, sub, MAIN), f32),
            pltpu.VMEM((16, NZ, sub, edge), f32),
            pltpu.VMEM((total - 1, sub, edge), f32),
            pltpu.VMEM((2 + NY + NX + NZ,) + loss.shape, f32),
            pltpu.VMEM(loss.shape, f32),
            dma((2,)), dma((2,)), dma((2,)),
            dma((32,)), dma((32,)), dma((32,)), dma((32,)), dma((4,)), dma((4,)),
            dma((8,)), dma((8,)), dma((6,)), dma((6,)), dma((16,)), dma((16,)), dma((total - 1,)), dma((total - 1,)),
            dma((14,)), dma((14,)),
        ],
        compiler_params=pltpu.CompilerParams(collective_id=1, has_side_effects=True, vmem_limit_bytes=63 << 20),
        name="reduce",
    )(shares, narrow, slots, loss)
    return out.reshape(2 * half, features), loss.reshape(())


def per_device(hidden, target, pool_table, pool_items, labels, chosen, offsets):
    user_count = lax.axis_size("users")
    factor = 1.0 / (user_count * (offsets.shape[1] - 1))
    table, both = gather(pool_table, pool_items, chosen[0])
    grad_hidden, loss, shares, narrow, slots = score(
        hidden[0], target[0], labels[0], both, offsets[0], table, factor
    )
    grad_table, loss_total = reduce_rows(shares, narrow, slots, loss)
    return (loss_total, grad_hidden[None], grad_table)


def solution(mesh):
    return jax.shard_map(
        per_device,
        mesh=mesh,
        in_specs=(
            P("users", "seq", None),
            P("users", "seq", None),
            P("users", None),
            P("users"),
            P("users", "seq"),
            P("users", "seq", None),
            P("users", None),
        ),
        out_specs=(P(), P("users", "seq", None), P("users", None)),
        check_vma=False,
    )
```
